32 devices in a mesh: seq: 8 (over z, core), dp: 4 (over y, x).
Axes of the slice: x: 2, y: 2, z: 4, core: 2. Of those that a mesh axis runs over, the one named last changes fastest.
Arguments:
- tokens: bfloat16 [8, 512, 768], P('dp', 'seq'), may hold values from -6 to 6
- segments: int32 [8, 512], P('dp', 'seq'), may hold values from 0 to 1, never falling along the last dimension, each value on 1 to 384 neighbouring positions
- padding: int32 [8, 512], P('dp', 'seq'), may hold values from 0 to 1, as said below
- w_qkv: bfloat16 [768, 2304], P(('seq', 'dp')), may hold values from -0.21875 to 0.21875
- w_out: bfloat16 [768, 768], P(('seq', 'dp')), may hold values from -0.625 to 0.625
- w_gate_up: bfloat16 [768, 6144], P(('seq', 'dp')), may hold values from -0.21875 to 0.21875
- w_down: bfloat16 [3072, 768], P(('seq', 'dp')), may hold values from -0.15625 to 0.15625
- biases: bfloat16 [4608], P(('seq', 'dp')), may hold values from -2 to 2
- norm_gains: bfloat16 [1536], P(('seq', 'dp')), may hold values from 0.25 to 1.75
- cotangent: bfloat16 [8, 512, 768], P('dp', 'seq'), may hold values from -6 to 6
Outputs:
- layer_out: bfloat16 [8, 512, 768], P('dp', 'seq')
- grad_tokens: float32 [8, 512, 768], P('dp', 'seq')
- grad_w_qkv: float32 [768, 2304], P(('seq', 'dp'))
- grad_w_out: float32 [768, 768], P(('seq', 'dp'))
- grad_w_gate_up: float32 [768, 6144], P(('seq', 'dp'))
- grad_w_down: float32 [3072, 768], P(('seq', 'dp'))
- grad_biases: float32 [4608], P(('seq', 'dp'))
- grad_norm_gains: float32 [1536], P(('seq', 'dp'))
The draws below stay inside these ranges and needn't reach their ends.
Inputs may be any that keep to these rules, and one draw needn't show every extreme that they name: `segments`: within a sequence the segment numbers never fall; each number 0 to 1 marks one document of 1 to 384 tokens. `padding`: in each sequence the zeros, if any, form its tail.
All inputs are finite; a program needn't handle non-finite values.
Results may differ from the reference program's by a relative error of at most 0.02.
Values may be sent and summed in bfloat16 or wider, within the bound.
No kernel may reach another device: no remote copies, remote signals or barrier semaphores. Data moves between devices by JAX's collectives and lax.ppermute only.
A program may use at most 128 MiB of HBM per device.

```python
import math
from functools import partial
import jax
import jax.numpy as jnp
import numpy as np
from jax import lax

D = 768
H = 12
HD = 64
FF = 3072
LENGTH = 512
SEQUENCES = 8
DOCS = 2
DOC_MOST = 384


def draw_padding(key, part):
    pad_count = jax.random.randint(key, (SEQUENCES, 1), 0, LENGTH // 8 + 1)
    positions = jnp.arange(LENGTH, dtype=jnp.int32)[None, :]
    return (positions < LENGTH - pad_count).astype(jnp.int32)


def level_of(own_key, dims, split, smallest, top_value):
    level = 1.0
    for dim, blocks in split:
        steps = jax.random.uniform(jax.random.fold_in(jax.random.fold_in(own_key, 6), dim), (blocks,), jnp.float32, smallest / len(split), top_value / len(split))
        level = level * jnp.repeat(jnp.exp(steps), dims[dim] // blocks).reshape((-1,) + (1,) * (len(dims) - 1 - dim))
    return level


def split_up(count, total, limit, lean):
    portions = [(1 << 20) // math.isqrt(rank ** lean) + 1 for rank in range(2, count + 1)]
    spare, given = total - limit - (count - 1), [1] * (count - 1)
    while spare > 0:
        free = [i for i in range(count - 1) if given[i] < limit]
        whole, budget = sum([portions[i] for i in free]), spare
        for i in free:
            more = min(limit - given[i], max(1, budget * portions[i] // whole), spare)
            given[i] = given[i] + more
            spare = spare - more
    return np.array([limit] + given)


def ragged(stream_key, count, total, reach, skew):
    if count == 2:
        one = jax.random.randint(stream_key, (), max(1, total - reach), min(reach, total - 1) + 1)
        return jnp.stack([one, total - one])
    sizes = jnp.asarray(split_up(count, total, reach, skew), jnp.int32)
    twos = (count - 1) // 2
    giver, sink = sizes[1:1 + 2 * twos:2], sizes[2:2 + 2 * twos:2]
    room = jnp.minimum(giver - 1, reach - sink)
    passed = jax.random.randint(jax.random.fold_in(stream_key, 1), (twos,), 0, 1 << 20) % (room + 1)
    sizes = sizes.at[1:1 + 2 * twos:2].set(giver - passed).at[2:2 + 2 * twos:2].set(sink + passed)
    return sizes[jax.random.permutation(jax.random.fold_in(stream_key, 2), count)]


def normal_values(stream_key, shape, spread, most, split=(), kind=jnp.bfloat16):
    loudness = level_of(stream_key, shape, split, -0.22, 0.18) if split else 1.0
    result = jax.random.normal(stream_key, shape, jnp.float32) * spread * loudness
    return jnp.minimum(jnp.maximum(result, -most), most).astype(kind)


def setup_inputs(seed: int = 0) -> dict:
    key_list = jax.random.split(jax.random.key(seed), 11)
    tokens = normal_values(key_list[0], (SEQUENCES, LENGTH, D), 1.0, 6.0, ((0, 4), (1, 8)))
    segments = jax.vmap(lambda own: jnp.searchsorted(jnp.cumsum(ragged(own, DOCS, LENGTH, DOC_MOST, 2)), jnp.arange(LENGTH), side="right"))(jax.random.split(key_list[1], SEQUENCES)).reshape((SEQUENCES, LENGTH)).astype(jnp.int32)
    padding = draw_padding(jax.random.fold_in(key_list[10], 71), 0)
    w_qkv = normal_values(key_list[3], (D, 3 * D), D ** -0.5, 0.21875, ((0, 32),))
    w_out = normal_values(key_list[4], (D, D), (D // 8) ** -0.5, 0.625, ((0, 32),))
    w_gate_up = normal_values(key_list[5], (D, 2 * FF), D ** -0.5, 0.21875, ((0, 32),))
    w_down = normal_values(key_list[6], (FF, D), (FF // 2) ** -0.5, 0.15625, ((0, 32),))
    biases = normal_values(key_list[7], (6 * D,), 0.3, 2.0, ((0, 32),))
    norm_gains = jnp.clip(1.0 + 0.15 * jax.random.normal(key_list[8], (2 * D,), jnp.float32), 0.25, 1.75).astype(jnp.bfloat16)
    cotangent = normal_values(key_list[9], (SEQUENCES, LENGTH, D), 1.0, 6.0, ((0, 4), (1, 8)))
    return {"tokens": tokens, "segments": segments, "padding": padding, "w_qkv": w_qkv, "w_out": w_out, "w_gate_up": w_gate_up, "w_down": w_down, "biases": biases, "norm_gains": norm_gains, "cotangent": cotangent}


NEG_FILL = -1e+30
EPSILON = 1e-12
HIGH = lax.Precision.HIGHEST

@jax.custom_vjp
def low(v):
    return lax.optimization_barrier(v.astype(jnp.bfloat16)).astype(jnp.float32)

@jax.custom_vjp
def low_back(v):
    return v

def low_keep(v):
    return (low(v), None)

def low_pass(kept, grad):
    return (grad,)

def back_keep(v):
    return (v, None)

def back_low(kept, grad):
    return (low(grad),)
low.defvjp(low_keep, low_pass)
low_back.defvjp(back_keep, back_low)

def slope_table(head_count):
    nearest = 2 ** int(math.floor(math.log2(head_count)))
    leading = [2.0 ** (-8.0 * (counter + 1) / nearest) for counter in range(nearest)]
    further = [2.0 ** (-8.0 * (counter + 1) / (2 * nearest)) for counter in range(2 * nearest)]
    return np.array(leading + further[0::2][:head_count - nearest], np.float32)

def matmul(left, right):
    return jnp.dot(left, right, precision=HIGH, preferred_element_type=jnp.float32)

def layer_norm(resid, norm_gain, norm_bias):
    centre = resid - lax.optimization_barrier(jnp.mean(resid, axis=-1, keepdims=True))
    inverse = lax.rsqrt(lax.optimization_barrier(jnp.mean(centre * centre, axis=-1, keepdims=True)) + EPSILON)
    return centre * inverse * norm_gain + norm_bias

def head_attention(packed, positions, allowed):
    query_head, key_head, value_head, slope = packed
    products = low_back(matmul(query_head, key_head.T) * 0.125)
    distance = jnp.abs(positions[:, None] - positions[None, :]).astype(jnp.float32)
    scores = jnp.where(allowed, products - slope * distance, NEG_FILL)
    top_score = lax.optimization_barrier(jnp.max(scores, axis=-1, keepdims=True))
    exponent = jnp.exp(scores - top_score)
    soft_rows = exponent / lax.optimization_barrier(jnp.sum(exponent, axis=-1, keepdims=True))
    return matmul(low(soft_rows), value_head)

def split_heads(matrix):
    return matrix.reshape(LENGTH, H, HD).transpose(1, 0, 2)

def sequence_layer(token_row, w_qkv, w_out, w_gate_up, w_down, biases, norm_gains, segment_row, valid_row):
    projected = low_back(matmul(low(token_row), w_qkv))
    queries = low(projected[:, :D] + biases[0:D])
    keys = low(projected[:, D:2 * D])
    values_all = low(projected[:, 2 * D:] + biases[D:2 * D])
    positions = jnp.arange(LENGTH)
    allowed = (segment_row[:, None] == segment_row[None, :]) & (valid_row[None, :] >= valid_row[:, None])
    slopes = jnp.asarray(slope_table(H))
    head_fn = jax.checkpoint(partial(head_attention, positions=positions, allowed=allowed))
    blended = lax.map(head_fn, (split_heads(queries), split_heads(keys), split_heads(values_all), slopes))
    attended = low(low_back(blended.transpose(1, 0, 2).reshape(LENGTH, D)))
    attn_proj = low_back(matmul(attended, w_out)) + biases[2 * D:3 * D]
    hidden_one = layer_norm(token_row + attn_proj, norm_gains[0:D], biases[4 * D:5 * D])
    gate_up = low_back(matmul(low(hidden_one), w_gate_up))
    activated = low(jax.nn.gelu(gate_up[:, :FF], approximate=False) * gate_up[:, FF:])
    mlp_out = low_back(matmul(activated, w_down)) + biases[3 * D:4 * D]
    output = layer_norm(hidden_one + mlp_out, norm_gains[D:2 * D], biases[5 * D:6 * D])
    return output * valid_row[:, None].astype(jnp.float32)

def reference(tokens, segments, padding, w_qkv, w_out, w_gate_up, w_down, biases, norm_gains, cotangent):
    weights = tuple((matrix.astype(jnp.float32) for matrix in (w_qkv, w_out, w_gate_up, w_down, biases, norm_gains)))

    def per_sequence(running, inputs):
        token_row, cotangent_row, segment_row, valid_row = inputs

        def forward(token_in, qkv_in, out_in, gate_in, down_in, bias_in, gain_in):
            return sequence_layer(token_in, qkv_in, out_in, gate_in, down_in, bias_in, gain_in, segment_row, valid_row)
        output, back_fn = jax.vjp(forward, token_row.astype(jnp.float32), *weights)
        gradients = back_fn(cotangent_row.astype(jnp.float32))
        running = tuple((earlier + piece for earlier, piece in zip(running, gradients[1:])))
        return (running, (output.astype(jnp.bfloat16), gradients[0]))
    initial = tuple((jnp.zeros_like(matrix) for matrix in weights))
    running, (layer_out, grad_tokens) = lax.scan(per_sequence, initial, (tokens, cotangent, segments, padding))
    return (layer_out, grad_tokens, running[0], running[1], running[2], running[3], running[4], running[5])
```

```python
import math

import jax
import jax.numpy as jnp
import numpy as np
from jax import lax
from jax.sharding import PartitionSpec as P

D = 768
H = 12
HD = 64
FF = 3072
GROUP = 4

NEG_FILL = -1e30
EPSILON = 1e-12
LOW = jnp.bfloat16
WIDE = jnp.float32


def slope_table(head_count):
    nearest = 2 ** int(math.floor(math.log2(head_count)))
    leading = [2.0 ** (-8.0 * (counter + 1) / nearest) for counter in range(nearest)]
    further = [2.0 ** (-8.0 * (counter + 1) / (2 * nearest)) for counter in range(2 * nearest)]
    return np.array(leading + further[0::2][: head_count - nearest], np.float32)


def dot(left, right):
    return jnp.dot(left, right, preferred_element_type=WIDE)


def dot_t(left, right):
    return lax.dot_general(left, right, (((1,), (1,)), ((), ())), preferred_element_type=WIDE)


def dot_w(left, right):
    return lax.dot_general(left, right, (((0,), (0,)), ((), ())), preferred_element_type=WIDE)


def swap(value, axis, size, mask):
    return lax.ppermute(value, axis, [(i, i ^ mask) for i in range(size)])


def put(buffer, value, index, axis):
    starts = [0] * buffer.ndim
    starts[axis] = index
    return lax.dynamic_update_slice(buffer, jnp.expand_dims(value, axis), starts)


def gather_by_swaps(value, name, size, place, axis, step=1):
    shape = value.shape[:axis] + (size,) + value.shape[axis:]
    result = put(jnp.zeros(shape, value.dtype), value, place, axis)
    total = lax.axis_size(name)
    for mask in range(1, size):
        result = put(result, swap(value, name, total, mask * step), place ^ mask, axis)
    return result


def scatter_by_swaps(value, name, size, place, axis, step=1):
    total = lax.axis_size(name)
    result = lax.dynamic_index_in_dim(value, place, axis, False)
    for mask in range(1, size):
        part = lax.dynamic_index_in_dim(value, place ^ mask, axis, False).astype(LOW)
        result = result + swap(part, name, total, mask * step).astype(WIDE)
    return result


def group_gather(rows, seq_count):
    partner = swap(rows, "seq", seq_count, 1)
    across = swap(rows, "seq", seq_count, 2)
    corner = swap(across, "seq", seq_count, 1)
    return jnp.concatenate([rows, partner, across, corner], axis=0)


def group_scatter(partial, seq_count):
    rows = partial.shape[0] // GROUP
    blocks = partial.reshape(GROUP, rows, partial.shape[1])
    sent = jnp.stack([blocks[1], blocks[3]]).astype(LOW)
    came = swap(sent, "seq", seq_count, 1).astype(WIDE)
    across = swap((blocks[2] + came[1]).astype(LOW), "seq", seq_count, 2).astype(WIDE)
    return blocks[0] + came[0] + across


def norm_forward(resid, norm_gain, norm_bias):
    centre = resid - jnp.mean(resid, axis=-1, keepdims=True)
    inverse = lax.rsqrt(jnp.mean(centre * centre, axis=-1, keepdims=True) + EPSILON)
    normed = centre * inverse
    return (normed * norm_gain + norm_bias, normed, inverse)


def norm_backward(grad_rows, normed, inverse, norm_gain):
    scaled = grad_rows * norm_gain
    first_mean = jnp.mean(scaled, axis=-1, keepdims=True)
    second_mean = jnp.mean(scaled * normed, axis=-1, keepdims=True)
    return inverse * (scaled - first_mean - normed * second_mean)


def geglu(gate_in, up_in):
    return jax.nn.gelu(gate_in, approximate=False) * up_in


def exchange(value):
    return lax.all_to_all(value, "seq", 0, 0)


def local(
    tokens, segments, padding, w_qkv, w_out, w_gate_up, w_down, biases, norm_gains, cotangent
):
    sequences, seq_rows = tokens.shape[:2]
    seq_count, dp_count = lax.axis_size("seq"), lax.axis_size("dp")
    seq_at, dp_at = lax.axis_index("seq"), lax.axis_index("dp")
    halves = seq_count // GROUP
    half_at, group_at = seq_at // GROUP, seq_at % GROUP
    rows = sequences * seq_rows
    length = seq_count * seq_rows
    head_groups = seq_count // sequences
    heads = -(-H // head_groups)
    padded = heads * head_groups
    width = heads * HD
    own_seq, own_heads = seq_at // head_groups, seq_at % head_groups
    wide_rows = w_qkv.shape[0]
    down_rows = w_down.shape[0]
    bias_part, gain_part = biases.shape[0], norm_gains.shape[0]
    run = dp_count * down_rows

    tokens_flat = tokens.reshape(rows, D)

    by_heads = w_qkv.reshape(wide_rows, 3, H, HD)
    by_heads = jnp.pad(by_heads, ((0, 0), (0, 0), (0, padded - H), (0, 0)))
    by_heads = by_heads.reshape(wide_rows, 3, head_groups, width).transpose(2, 0, 1, 3)
    by_heads = by_heads.reshape(1, head_groups, wide_rows, 3 * width)
    by_heads = jnp.broadcast_to(by_heads, (sequences,) + by_heads.shape[1:])
    qkv_rows = exchange(by_heads.reshape(seq_count, wide_rows, 3 * width))
    qkv_own = gather_by_swaps(qkv_rows, "dp", dp_count, dp_at, 1).reshape(D, 3 * width)

    small = jnp.concatenate([biases, norm_gains])
    small_all = gather_by_swaps(small, "dp", dp_count, dp_at, 0).reshape(-1)
    marks = jnp.concatenate([segments.reshape(-1), padding.reshape(-1)]).astype(LOW)
    flat = jnp.concatenate([small_all, marks])
    extra_rows = -(-flat.shape[0] // (8 * D)) * 8
    flat = jnp.pad(flat, (0, extra_rows * D - flat.shape[0])).reshape(extra_rows, D)
    packed = jnp.concatenate([tokens_flat, flat], axis=0)
    line = lax.all_gather(packed, "seq", axis=0, tiled=False)
    token_rows = lax.dynamic_slice_in_dim(line[:, :rows], own_seq * seq_rows, seq_rows, 1)
    token_rows = token_rows.reshape(length, D)
    small_line = line[:, rows:].reshape(seq_count, extra_rows * D)
    vectors = small_line[:, : small_all.shape[0]].reshape(
        seq_count, dp_count, bias_part + gain_part
    )
    bias_vector = vectors[:, :, :bias_part].reshape(6 * D).astype(WIDE)
    gain_vector = vectors[:, :, bias_part:].reshape(2 * D).astype(WIDE)
    mark_line = small_line[:, small_all.shape[0] : small_all.shape[0] + 2 * rows]
    mark_line = mark_line.reshape(seq_count, 2, sequences, seq_rows)
    mark_line = lax.dynamic_index_in_dim(mark_line, own_seq, 2, False).astype(WIDE)
    own_segments = mark_line[:, 0].reshape(length)
    own_valid = mark_line[:, 1].reshape(length)

    out_part = gather_by_swaps(w_out, "dp", dp_count, dp_at, 0).reshape(-1, D)
    out_full = lax.all_gather(out_part, "seq", axis=0, tiled=True)

    columns = w_gate_up.reshape(wide_rows, 2, halves, GROUP, run).transpose(3, 0, 1, 2, 4)
    columns = columns.reshape(1, GROUP, wide_rows, 2 * halves * run)
    columns = jnp.broadcast_to(columns, (halves,) + columns.shape[1:])
    hidden = halves * run
    gate_up_rows = exchange(columns.reshape(seq_count, wide_rows, 2 * hidden))
    gate_up_own = gather_by_swaps(gate_up_rows, "dp", dp_count, dp_at, 1).reshape(D, 2 * hidden)
    down_part = gather_by_swaps(w_down, "seq", halves, half_at, 0, GROUP)
    down_own = gather_by_swaps(down_part, "dp", dp_count, dp_at, 1).reshape(hidden, D)

    def own_part(vector):
        spread = jnp.pad(vector, (0, padded * HD - D))
        return lax.dynamic_slice_in_dim(spread, own_heads * width, width, 0)

    projected = dot(token_rows, qkv_own)
    queries = (projected[:, :width] + own_part(bias_vector[0:D])).astype(LOW)
    keys = projected[:, width : 2 * width].astype(LOW)
    values = (projected[:, 2 * width :] + own_part(bias_vector[D : 2 * D])).astype(LOW)
    queries, keys, values = (
        part.reshape(length, heads, HD).transpose(1, 0, 2) for part in (queries, keys, values)
    )
    slopes = jnp.pad(jnp.asarray(slope_table(H)), (0, padded - H))
    slopes = lax.dynamic_slice_in_dim(slopes, own_heads * heads, heads, 0)
    position = jnp.arange(length, dtype=jnp.int32)
    distance = jnp.abs(position[:, None] - position[None, :]).astype(WIDE)
    allowed = (own_segments[:, None] == own_segments[None, :]) & (
        own_valid[None, :] >= own_valid[:, None]
    )
    products = jnp.einsum("hqd,hkd->hqk", queries, keys, preferred_element_type=WIDE) * 0.125
    scores = jnp.where(
        allowed[None], products - slopes[:, None, None] * distance[None], NEG_FILL
    )
    top_score = jnp.max(scores, axis=-1, keepdims=True)
    exponent = jnp.exp(scores - top_score)
    soft = exponent / jnp.sum(exponent, axis=-1, keepdims=True)
    soft_low = soft.astype(LOW)
    blended = jnp.einsum("hqk,hkd->qhd", soft_low, values, preferred_element_type=WIDE)
    blended = blended.astype(LOW).reshape(seq_count, seq_rows, width)

    def to_rows(by_head):
        arrived = exchange(by_head).reshape(sequences, head_groups, seq_rows, -1, width)
        arrived = arrived.transpose(0, 2, 3, 1, 4).reshape(rows, -1, padded * HD)
        return arrived[:, :, :D].reshape(rows, -1)

    attended = to_rows(blended)
    token_wide = tokens_flat.astype(WIDE)
    resid_one = token_wide + (dot(attended, out_full) + bias_vector[2 * D : 3 * D])
    hidden_one, normed_one, inverse_one = norm_forward(
        resid_one, gain_vector[0:D], bias_vector[4 * D : 5 * D]
    )
    hidden_rows = group_gather(hidden_one.astype(LOW), seq_count)
    gate_up = dot(hidden_rows, gate_up_own)
    activated_wide, geglu_back = jax.vjp(geglu, gate_up[:, :hidden], gate_up[:, hidden:])
    activated = activated_wide.astype(LOW)
    mlp_out = group_scatter(dot(activated, down_own), seq_count)
    resid_two = hidden_one + (mlp_out + bias_vector[3 * D : 4 * D])
    normed_out, normed_two, inverse_two = norm_forward(
        resid_two, gain_vector[D : 2 * D], bias_vector[5 * D : 6 * D]
    )
    valid_mask = padding.reshape(rows, 1).astype(WIDE)
    layer_out = (normed_out * valid_mask).astype(LOW)

    grad_final = cotangent.reshape(rows, D).astype(WIDE) * valid_mask
    grad_gain_two = jnp.sum(grad_final * normed_two, axis=0)
    grad_bias_two = jnp.sum(grad_final, axis=0)
    grad_resid_two = norm_backward(grad_final, normed_two, inverse_two, gain_vector[D : 2 * D])
    grad_bias_down = jnp.sum(grad_resid_two, axis=0)
    grad_mlp_rows = group_gather(grad_resid_two.astype(LOW), seq_count)
    grad_activated = dot_t(grad_mlp_rows, down_own)
    grad_gate, grad_up = geglu_back(grad_activated)
    grad_gate_up_low = jnp.concatenate([grad_gate, grad_up], axis=-1).astype(LOW)
    grad_hidden = grad_resid_two + group_scatter(dot_t(grad_gate_up_low, gate_up_own), seq_count)
    grad_down = dot_w(activated, grad_mlp_rows)
    grad_gate_up = dot_w(hidden_rows, grad_gate_up_low)

    grad_gain_one = jnp.sum(grad_hidden * normed_one, axis=0)
    grad_bias_one = jnp.sum(grad_hidden, axis=0)
    grad_resid_one = norm_backward(grad_hidden, normed_one, inverse_one, gain_vector[0:D])
    grad_bias_attn = jnp.sum(grad_resid_one, axis=0)
    grad_attn_low = grad_resid_one.astype(LOW)
    grad_attended = dot_t(grad_attn_low, out_full).astype(LOW)
    grad_out_w = dot_w(attended, grad_attn_low)

    spread = grad_attended.reshape(sequences, seq_rows, D)
    spread = jnp.pad(spread, ((0, 0), (0, 0), (0, padded * HD - D)))
    spread = spread.reshape(sequences, seq_rows, head_groups, width).transpose(0, 2, 1, 3)
    grad_blended = exchange(spread.reshape(seq_count, seq_rows, width))
    grad_blended = grad_blended.reshape(length, heads, HD).transpose(1, 0, 2)
    grad_soft = jnp.einsum("hqd,hkd->hqk", grad_blended, values, preferred_element_type=WIDE)
    delta = jnp.sum(soft * grad_soft, axis=-1, keepdims=True)
    grad_scores = (soft * (grad_soft - delta)).astype(LOW)
    grad_queries = jnp.einsum("hqk,hkd->qhd", grad_scores, keys, preferred_element_type=WIDE)
    grad_keys = jnp.einsum("hqk,hqd->khd", grad_scores, queries, preferred_element_type=WIDE)
    grad_values = jnp.einsum("hqk,hqd->khd", soft_low, grad_blended, preferred_element_type=WIDE)
    grad_queries = grad_queries.reshape(length, width) * 0.125
    grad_keys = grad_keys.reshape(length, width) * 0.125
    grad_values = grad_values.reshape(length, width)

    def whole_part(vector):
        spread = jnp.zeros((padded * HD,), WIDE)
        return lax.dynamic_update_slice(spread, vector, (own_heads * width,))[:D]

    grad_bias_query = whole_part(jnp.sum(grad_queries, axis=0))
    grad_bias_value = whole_part(jnp.sum(grad_values, axis=0))
    grad_proj = jnp.concatenate([grad_queries, grad_keys, grad_values], axis=-1).astype(LOW)
    qkv_full = lax.all_gather(w_qkv, ("seq", "dp"), axis=0, tiled=True)
    grad_rows = to_rows(grad_proj.reshape(seq_count, seq_rows * 3, width))
    grad_tokens = grad_resid_one + dot_t(grad_rows, qkv_full)
    grad_qkv = dot_w(token_rows, grad_proj)

    early = jnp.concatenate(
        [
            grad_gate_up.reshape(seq_count, dp_count, wide_rows, 2 * hidden),
            grad_out_w.reshape(seq_count, dp_count, wide_rows, D),
        ],
        axis=-1,
    )
    early = scatter_by_swaps(early, "dp", dp_count, dp_at, 1).astype(LOW)
    early = exchange(early).astype(WIDE)
    shard_out = jnp.sum(early[:, :, 2 * hidden :], axis=0)
    shard_gate_up = early[:, :, : 2 * hidden].reshape(halves, GROUP, wide_rows, 2 * hidden)
    shard_gate_up = jnp.sum(shard_gate_up, axis=0).reshape(GROUP, wide_rows, 2, halves, run)
    shard_gate_up = shard_gate_up.transpose(1, 2, 3, 0, 4).reshape(wide_rows, 2 * FF)
    shard_down = grad_down.reshape(halves, dp_count, down_rows, D)
    shard_down = scatter_by_swaps(shard_down, "dp", dp_count, dp_at, 1)
    shard_down = scatter_by_swaps(shard_down, "seq", halves, half_at, 0, GROUP)

    grad_biases = jnp.concatenate(
        [
            grad_bias_query,
            grad_bias_value,
            grad_bias_attn,
            grad_bias_down,
            grad_bias_one,
            grad_bias_two,
        ]
    ).reshape(seq_count, dp_count, bias_part)
    grad_gains = jnp.concatenate([grad_gain_one, grad_gain_two])
    grad_gains = grad_gains.reshape(seq_count, dp_count, gain_part)
    grad_small = jnp.concatenate([grad_biases, grad_gains], axis=-1)
    small_columns = (bias_part + gain_part) // wide_rows
    grad_small = grad_small.reshape(seq_count, dp_count, wide_rows, small_columns)
    late = jnp.concatenate(
        [grad_qkv.reshape(seq_count, dp_count, wide_rows, 3 * width), grad_small], axis=-1
    )
    late = scatter_by_swaps(late, "dp", dp_count, dp_at, 1).astype(LOW)
    late = exchange(late).astype(WIDE)
    shard_small = jnp.sum(late[:, :, 3 * width :], axis=0).reshape(-1)
    shard_qkv = late[:, :, : 3 * width].reshape(sequences, head_groups, wide_rows, 3, width)
    shard_qkv = jnp.sum(shard_qkv, axis=0).transpose(1, 2, 0, 3)
    shard_qkv = shard_qkv.reshape(wide_rows, 3, padded * HD)[:, :, :D].reshape(wide_rows, 3 * D)

    shape = (sequences, seq_rows, D)
    return (
        layer_out.reshape(shape),
        grad_tokens.reshape(shape),
        shard_qkv,
        shard_out,
        shard_gate_up,
        shard_down,
        shard_small[:bias_part],
        shard_small[bias_part:],
    )


def solution(mesh):
    in_specs = (
        P("dp", "seq", None),
        P("dp", "seq"),
        P("dp", "seq"),
        P(("seq", "dp"), None),
        P(("seq", "dp"), None),
        P(("seq", "dp"), None),
        P(("seq", "dp"), None),
        P(("seq", "dp")),
        P(("seq", "dp")),
        P("dp", "seq", None),
    )
    out_specs = (
        P("dp", "seq", None),
        P("dp", "seq", None),
        P(("seq", "dp"), None),
        P(("seq", "dp"), None),
        P(("seq", "dp"), None),
        P(("seq", "dp"), None),
        P(("seq", "dp")),
        P(("seq", "dp")),
    )
    return jax.shard_map(local, mesh=mesh, in_specs=in_specs, out_specs=out_specs, check_vma=False)
```

```python
import math

import jax
import jax.numpy as jnp
import numpy as np
from jax import lax
from jax.experimental import pallas as pl
from jax.experimental.pallas import tpu as pltpu
from jax.sharding import PartitionSpec as P


D = 768
H = 12
HD = 64
FF = 3072
GROUP = 4
QUERY_BLOCK = 128

NEG_FILL = -1e30
EPSILON = 1e-12
LOW = jnp.bfloat16
WIDE = jnp.float32


def slope_table(head_count):
    nearest = 2 ** int(math.floor(math.log2(head_count)))
    leading = [2.0 ** (-8.0 * (counter + 1) / nearest) for counter in range(nearest)]
    further = [2.0 ** (-8.0 * (counter + 1) / (2 * nearest)) for counter in range(2 * nearest)]
    return np.array(leading + further[0::2][: head_count - nearest], np.float32)


def dot(left, right):
    return jnp.dot(left, right, preferred_element_type=WIDE)


def dot_t(left, right):
    return lax.dot_general(left, right, (((1,), (1,)), ((), ())), preferred_element_type=WIDE)


def dot_w(left, right):
    return lax.dot_general(left, right, (((0,), (0,)), ((), ())), preferred_element_type=WIDE)


def swap(value, axis, size, mask):
    return lax.ppermute(value, axis, [(i, i ^ mask) for i in range(size)])


def put(buffer, value, index, axis):
    starts = [0] * buffer.ndim
    starts[axis] = index
    return lax.dynamic_update_slice(buffer, jnp.expand_dims(value, axis), starts)


def swapped(value, name, size, step=1):
    total = lax.axis_size(name)
    return (value,) + tuple(swap(value, name, total, mask * step) for mask in range(1, size))


def in_order(pieces, place, axis):
    value = pieces[0]
    shape = value.shape[:axis] + (len(pieces),) + value.shape[axis:]
    result = jnp.zeros(shape, value.dtype)
    for mask, piece in enumerate(pieces):
        result = put(result, piece, place ^ mask, axis)
    return result


def gather_by_swaps(value, name, size, place, axis, step=1):
    return in_order(swapped(value, name, size, step), place, axis)


def scatter_swaps(value, name, size, place, axis, step=1):
    total = lax.axis_size(name)
    pieces = [lax.dynamic_index_in_dim(value, place, axis, False)]
    for mask in range(1, size):
        part = lax.dynamic_index_in_dim(value, place ^ mask, axis, False).astype(LOW)
        pieces.append(swap(part, name, total, mask * step))
    return tuple(pieces)


def add_up(pieces):
    result = pieces[0].astype(WIDE)
    for piece in pieces[1:]:
        result = result + piece.astype(WIDE)
    return result


def scatter_by_swaps(value, name, size, place, axis, step=1):
    return add_up(scatter_swaps(value, name, size, place, axis, step))


def group_gather(rows, seq_count):
    partner = swap(rows, "seq", seq_count, 1)
    across = swap(rows, "seq", seq_count, 2)
    corner = swap(across, "seq", seq_count, 1)
    return jnp.concatenate([rows, partner, across, corner], axis=0)


def group_scatter(partial, seq_count):
    rows = partial.shape[0] // GROUP
    blocks = partial.reshape(GROUP, rows, partial.shape[1])
    sent = jnp.stack([blocks[1], blocks[3]]).astype(LOW)
    came = swap(sent, "seq", seq_count, 1).astype(WIDE)
    across = swap((blocks[2] + came[1]).astype(LOW), "seq", seq_count, 2).astype(WIDE)
    return blocks[0] + came[0] + across


def sequence_reduce(blocks, seq_count, seq_at, sequences):
    total, step = blocks, 1
    while total.shape[0] > sequences:
        halves = total.reshape((total.shape[0] // 2, 2) + total.shape[1:])
        bit = (seq_at // step) % 2
        sent = lax.dynamic_index_in_dim(halves, 1 - bit, 1, False).astype(LOW)
        kept = lax.dynamic_index_in_dim(halves, bit, 1, False).astype(WIDE)
        total = kept + swap(sent, "seq", seq_count, step).astype(WIDE)
        step *= 2
    return total


def sequence_swap(total, seq_count, seq_at, sequences):
    step = seq_count // sequences
    own = seq_at // step
    result = put(jnp.zeros_like(total), lax.dynamic_index_in_dim(total, own, 0, False), own, 0)
    for mask in range(1, sequences):
        sent = lax.dynamic_index_in_dim(total, own ^ mask, 0, False).astype(LOW)
        came = swap(sent, "seq", seq_count, mask * step).astype(WIDE)
        result = put(result, came, own ^ mask, 0)
    return result


def head_columns(head, width):
    column = lax.broadcasted_iota(jnp.int32, (1, width), 1)
    return ((column >= head * HD) & (column < (head + 1) * HD)).astype(WIDE).astype(LOW)


def block_scores(query_rows, keys, slope, start, marks_column, marks_row):
    shape = (query_rows.shape[0], keys.shape[0])
    row = lax.broadcasted_iota(jnp.int32, shape, 0) + start
    column = lax.broadcasted_iota(jnp.int32, shape, 1)
    distance = jnp.abs(row - column).astype(WIDE)
    allowed = (marks_column[:, 0:1] == marks_row[0:1]) & (marks_row[1:2] >= marks_column[:, 1:2])
    return jnp.where(allowed, dot_t(query_rows, keys) * 0.125 - slope * distance, NEG_FILL)


def attend_kernel(heads, width, slopes, qkv, marks_column, marks_row, out, sums):
    keys, values = qkv[:, width : 2 * width], qkv[:, 2 * width :]

    def block(index, carry):
        start = pl.multiple_of(index * QUERY_BLOCK, QUERY_BLOCK)
        here = pl.ds(start, QUERY_BLOCK)
        queries, marks = qkv[here, :width], marks_column[here, :]
        blended = jnp.zeros((QUERY_BLOCK, width), WIDE)
        for head in range(heads):
            mask = head_columns(head, width)
            scores = block_scores(queries * mask, keys, slopes[head], start, marks, marks_row[...])
            top_score = jnp.max(scores, axis=-1, keepdims=True)
            exponent = jnp.exp(scores - top_score)
            total = jnp.sum(exponent, axis=-1, keepdims=True)
            blended = blended + dot((exponent / total).astype(LOW), values * mask)
            sums[here, head : head + 1] = top_score + jnp.log(total)
        out[here, :] = blended.astype(LOW)
        return carry

    lax.fori_loop(0, qkv.shape[0] // QUERY_BLOCK, block, 0)


def attend_back_kernel(
    heads, width, slopes, qkv, grad_out, sums, marks_column, marks_row, grad_proj, totals, acc
):
    keys, values = qkv[:, width : 2 * width], qkv[:, 2 * width :]
    acc[...] = jnp.zeros(acc.shape, WIDE)
    totals[...] = jnp.zeros(totals.shape, WIDE)

    def block(index, carry):
        start = pl.multiple_of(index * QUERY_BLOCK, QUERY_BLOCK)
        here = pl.ds(start, QUERY_BLOCK)
        queries, marks, grads = qkv[here, :width], marks_column[here, :], grad_out[here, :]
        grad_query = jnp.zeros((QUERY_BLOCK, width), WIDE)
        grad_key = jnp.zeros((qkv.shape[0], width), WIDE)
        grad_value = jnp.zeros((qkv.shape[0], width), WIDE)
        for head in range(heads):
            mask = head_columns(head, width)
            own_query, own_grad = queries * mask, grads * mask
            scores = block_scores(own_query, keys, slopes[head], start, marks, marks_row[...])
            soft = jnp.exp(scores - sums[here, head : head + 1])
            grad_soft = dot_t(own_grad, values)
            delta = jnp.sum(soft * grad_soft, axis=-1, keepdims=True)
            grad_scores = (soft * (grad_soft - delta)).astype(LOW)
            grad_query = grad_query + dot(grad_scores, keys * mask)
            grad_key = grad_key + dot_w(grad_scores, own_query)
            grad_value = grad_value + dot_w(soft.astype(LOW), own_grad)
        grad_query = grad_query * 0.125
        grad_proj[here, :width] = grad_query.astype(LOW)
        totals[0:1] = totals[0:1] + jnp.sum(grad_query, axis=0, keepdims=True)
        acc[0] = acc[0] + grad_key
        acc[1] = acc[1] + grad_value
        return carry

    lax.fori_loop(0, qkv.shape[0] // QUERY_BLOCK, block, 0)
    grad_proj[:, width : 2 * width] = (acc[0] * 0.125).astype(LOW)
    grad_proj[:, 2 * width :] = acc[1].astype(LOW)
    totals[1:2] = jnp.sum(acc[1], axis=0, keepdims=True)


def attend(heads, width, slopes, qkv, marks_column, marks_row):
    length = qkv.shape[0]
    return pl.pallas_call(
        lambda *refs: attend_kernel(heads, width, *refs),
        out_shape=(
            jax.ShapeDtypeStruct((length, width), LOW),
            jax.ShapeDtypeStruct((length, heads), WIDE),
        ),
        in_specs=[pl.BlockSpec(memory_space=pltpu.SMEM)]
        + [pl.BlockSpec(memory_space=pltpu.VMEM)] * 3,
        out_specs=[pl.BlockSpec(memory_space=pltpu.VMEM)] * 2,
        name="attend",
    )(slopes, qkv, marks_column, marks_row)


def attend_back(heads, width, slopes, qkv, grad_out, sums, marks_column, marks_row):
    length = qkv.shape[0]
    return pl.pallas_call(
        lambda *refs: attend_back_kernel(heads, width, *refs),
        out_shape=(
            jax.ShapeDtypeStruct((length, 3 * width), LOW),
            jax.ShapeDtypeStruct((8, width), WIDE),
        ),
        in_specs=[pl.BlockSpec(memory_space=pltpu.SMEM)]
        + [pl.BlockSpec(memory_space=pltpu.VMEM)] * 5,
        out_specs=[pl.BlockSpec(memory_space=pltpu.VMEM)] * 2,
        scratch_shapes=[pltpu.VMEM((2, length, width), WIDE)],
        name="attend_back",
    )(slopes, qkv, grad_out, sums, marks_column, marks_row)


def norm_forward(resid, norm_gain, norm_bias):
    centre = resid - jnp.mean(resid, axis=-1, keepdims=True)
    inverse = lax.rsqrt(jnp.mean(centre * centre, axis=-1, keepdims=True) + EPSILON)
    normed = centre * inverse
    return (normed * norm_gain + norm_bias, normed, inverse)


def norm_backward(grad_rows, normed, inverse, norm_gain):
    scaled = grad_rows * norm_gain
    first_mean = jnp.mean(scaled, axis=-1, keepdims=True)
    second_mean = jnp.mean(scaled * normed, axis=-1, keepdims=True)
    return inverse * (scaled - first_mean - normed * second_mean)


def geglu(gate_in, up_in):
    return jax.nn.gelu(gate_in, approximate=False) * up_in


def exchange(value):
    return lax.all_to_all(value, "seq", 0, 0)


def together(*values):
    return lax.optimization_barrier(values)


def local(
    tokens, segments, padding, w_qkv, w_out, w_gate_up, w_down, biases, norm_gains, cotangent
):
    sequences, seq_rows = tokens.shape[:2]
    seq_count, dp_count = lax.axis_size("seq"), lax.axis_size("dp")
    seq_at, dp_at = lax.axis_index("seq"), lax.axis_index("dp")
    halves = seq_count // GROUP
    half_at = seq_at // GROUP
    rows = sequences * seq_rows
    length = seq_count * seq_rows
    head_groups = seq_count // sequences
    heads = -(-H // head_groups)
    padded = heads * head_groups
    width = heads * HD
    own_seq, own_heads = seq_at // head_groups, seq_at % head_groups
    wide_rows = w_qkv.shape[0]
    down_rows = w_down.shape[0]
    bias_part, gain_part = biases.shape[0], norm_gains.shape[0]
    run = dp_count * down_rows

    tokens_flat = tokens.reshape(rows, D)

    by_heads = w_qkv.reshape(wide_rows, 3, H, HD)
    by_heads = jnp.pad(by_heads, ((0, 0), (0, 0), (0, padded - H), (0, 0)))
    by_heads = by_heads.reshape(wide_rows, 3, head_groups, width).transpose(2, 0, 1, 3)
    by_heads = by_heads.reshape(1, head_groups, wide_rows, 3 * width)
    by_heads = jnp.broadcast_to(by_heads, (sequences,) + by_heads.shape[1:])
    by_heads = by_heads.reshape(seq_count, wide_rows, 3 * width)
    small_columns = (bias_part + gain_part) // wide_rows
    small = jnp.concatenate([biases, norm_gains]).reshape(1, wide_rows, small_columns)
    small = jnp.broadcast_to(small, (seq_count, wide_rows, small_columns))
    qkv_rows = exchange(jnp.concatenate([by_heads, small], axis=-1))
    qkv_rows, gate_up_in, down_in = together(qkv_rows, w_gate_up, w_down)
    qkv_own = gather_by_swaps(qkv_rows, "dp", dp_count, dp_at, 1)

    marks = jnp.concatenate([segments.reshape(-1), padding.reshape(-1)]).astype(LOW)
    extra_rows = -(-marks.shape[0] // (8 * D)) * 8
    marks = jnp.pad(marks, (0, extra_rows * D - marks.shape[0])).reshape(extra_rows, D)
    packed = jnp.concatenate([tokens_flat, marks], axis=0)
    line = lax.all_gather(packed, "seq", axis=0, tiled=False)
    token_rows = lax.dynamic_slice_in_dim(line[:, :rows], own_seq * seq_rows, seq_rows, 1)
    token_rows = token_rows.reshape(length, D)
    mark_line = line[:, rows:].reshape(seq_count, extra_rows * D)[:, : 2 * rows]
    mark_line = mark_line.reshape(seq_count, 2, sequences, seq_rows)
    mark_line = lax.dynamic_index_in_dim(mark_line, own_seq, 2, False).astype(WIDE)
    marks_row = jnp.stack([mark_line[:, 0].reshape(length), mark_line[:, 1].reshape(length)])
    marks_column = marks_row.T

    out_part = gather_by_swaps(w_out, "dp", dp_count, dp_at, 0).reshape(-1, D)
    out_full = lax.all_gather(out_part, "seq", axis=0, tiled=True)

    columns = gate_up_in.reshape(wide_rows, 2, halves, GROUP, run).transpose(3, 0, 1, 2, 4)
    columns = columns.reshape(1, GROUP, wide_rows, 2 * halves * run)
    columns = jnp.broadcast_to(columns, (halves,) + columns.shape[1:])
    hidden = halves * run
    gate_up_rows = exchange(columns.reshape(seq_count, wide_rows, 2 * hidden))
    gate_up_pieces = swapped(gate_up_rows, "dp", dp_count)
    down_part = gather_by_swaps(down_in, "seq", halves, half_at, 0, GROUP)
    down_pieces = swapped(down_part, "dp", dp_count)

    vectors = qkv_own[..., 3 * width :].reshape(seq_count, dp_count, bias_part + gain_part)
    bias_vector = vectors[:, :, :bias_part].reshape(6 * D).astype(WIDE)
    gain_vector = vectors[:, :, bias_part:].reshape(2 * D).astype(WIDE)
    qkv_own = qkv_own[..., : 3 * width].reshape(D, 3 * width)

    def own_part(vector):
        spread = jnp.pad(vector, (0, padded * HD - D))
        return lax.dynamic_slice_in_dim(spread, own_heads * width, width, 0)

    own_bias = jnp.concatenate(
        [own_part(bias_vector[0:D]), jnp.zeros((width,), WIDE), own_part(bias_vector[D : 2 * D])]
    )
    qkv = (dot(token_rows, qkv_own) + own_bias).astype(LOW)
    slopes = jnp.pad(jnp.asarray(slope_table(H)), (0, padded - H))
    slopes = lax.dynamic_slice_in_dim(slopes, own_heads * heads, heads, 0)
    blended, log_sums = attend(heads, width, slopes, qkv, marks_column, marks_row)
    blended = blended.reshape(seq_count, seq_rows, width)

    def to_rows(by_head):
        arrived = exchange(by_head).reshape(sequences, head_groups, seq_rows, -1, width)
        arrived = arrived.transpose(0, 2, 3, 1, 4).reshape(rows, -1, padded * HD)
        return arrived[:, :, :D].reshape(rows, -1)

    attended = to_rows(blended)
    token_wide = tokens_flat.astype(WIDE)
    resid_one = token_wide + (dot(attended, out_full) + bias_vector[2 * D : 3 * D])
    resid_one, gate_up_pieces, down_pieces = together(resid_one, gate_up_pieces, down_pieces)
    gate_up_own = in_order(gate_up_pieces, dp_at, 1).reshape(D, 2 * hidden)
    down_own = in_order(down_pieces, dp_at, 1).reshape(hidden, D)
    hidden_one, normed_one, inverse_one = norm_forward(
        resid_one, gain_vector[0:D], bias_vector[4 * D : 5 * D]
    )
    hidden_rows = group_gather(hidden_one.astype(LOW), seq_count)
    gate_up = dot(hidden_rows, gate_up_own)
    activated_wide, geglu_back = jax.vjp(geglu, gate_up[:, :hidden], gate_up[:, hidden:])
    activated = activated_wide.astype(LOW)
    mlp_out = group_scatter(dot(activated, down_own), seq_count)
    resid_two = hidden_one + (mlp_out + bias_vector[3 * D : 4 * D])
    normed_out, normed_two, inverse_two = norm_forward(
        resid_two, gain_vector[D : 2 * D], bias_vector[5 * D : 6 * D]
    )
    valid_mask = padding.reshape(rows, 1).astype(WIDE)
    layer_out = (normed_out * valid_mask).astype(LOW)

    grad_final = cotangent.reshape(rows, D).astype(WIDE) * valid_mask
    grad_gain_two = jnp.sum(grad_final * normed_two, axis=0)
    grad_bias_two = jnp.sum(grad_final, axis=0)
    grad_resid_two = norm_backward(grad_final, normed_two, inverse_two, gain_vector[D : 2 * D])
    grad_bias_down = jnp.sum(grad_resid_two, axis=0)
    grad_mlp_rows = group_gather(grad_resid_two.astype(LOW), seq_count)
    grad_activated = dot_t(grad_mlp_rows, down_own)
    grad_gate, grad_up = geglu_back(grad_activated)
    grad_gate_up_low = jnp.concatenate([grad_gate, grad_up], axis=-1).astype(LOW)
    grad_hidden = grad_resid_two + group_scatter(dot_t(grad_gate_up_low, gate_up_own), seq_count)
    grad_down = dot_w(activated, grad_mlp_rows)
    grad_gate_up = dot_w(hidden_rows, grad_gate_up_low)
    grad_gate_up = grad_gate_up.reshape(seq_count, dp_count, wide_rows, 2 * hidden)
    grad_gate_up = scatter_swaps(grad_gate_up, "dp", dp_count, dp_at, 1)
    shard_down = grad_down.reshape(halves, dp_count, down_rows, D)
    shard_down = scatter_by_swaps(shard_down, "dp", dp_count, dp_at, 1)
    shard_down = scatter_by_swaps(shard_down, "seq", halves, half_at, 0, GROUP)

    grad_gain_one = jnp.sum(grad_hidden * normed_one, axis=0)
    grad_bias_one = jnp.sum(grad_hidden, axis=0)
    grad_resid_one = norm_backward(grad_hidden, normed_one, inverse_one, gain_vector[0:D])
    grad_bias_attn = jnp.sum(grad_resid_one, axis=0)
    grad_attn_low = grad_resid_one.astype(LOW)
    grad_attended = dot_t(grad_attn_low, out_full).astype(LOW)
    grad_out_w = dot_w(attended, grad_attn_low)
    grad_out_w = grad_out_w.reshape(seq_count, dp_count, wide_rows, D)
    grad_out_w = scatter_by_swaps(grad_out_w, "dp", dp_count, dp_at, 1).astype(LOW)

    spread = grad_attended.reshape(sequences, seq_rows, D)
    spread = jnp.pad(spread, ((0, 0), (0, 0), (0, padded * HD - D)))
    spread = spread.reshape(sequences, seq_rows, head_groups, width).transpose(0, 2, 1, 3)
    grad_blended = exchange(spread.reshape(seq_count, seq_rows, width))
    grad_blended, grad_gate_up = together(grad_blended, grad_gate_up)
    grad_gate_up = add_up(grad_gate_up).astype(LOW)
    grad_blended = grad_blended.reshape(length, width)
    grad_proj, totals = attend_back(
        heads, width, slopes, qkv, grad_blended, log_sums, marks_column, marks_row
    )

    def whole_part(vector):
        spread = jnp.zeros((padded * HD,), WIDE)
        return lax.dynamic_update_slice(spread, vector, (own_heads * width,))[:D]

    grad_bias_query = whole_part(totals[0])
    grad_bias_value = whole_part(totals[1])
    grad_rows = dot_t(grad_proj, qkv_own).astype(LOW).reshape(seq_count, seq_rows, D)
    grad_rows = sequence_reduce(grad_rows, seq_count, seq_at, sequences)
    grad_qkv = dot_w(token_rows, grad_proj)

    early = exchange(grad_gate_up).astype(WIDE)
    shard_gate_up = early.reshape(halves, GROUP, wide_rows, 2 * hidden)
    shard_gate_up = jnp.sum(shard_gate_up, axis=0).reshape(GROUP, wide_rows, 2, halves, run)
    shard_gate_up = shard_gate_up.transpose(1, 2, 3, 0, 4).reshape(wide_rows, 2 * FF)

    grad_biases = jnp.concatenate(
        [
            grad_bias_query,
            grad_bias_value,
            grad_bias_attn,
            grad_bias_down,
            grad_bias_one,
            grad_bias_two,
        ]
    ).reshape(seq_count, dp_count, bias_part)
    grad_gains = jnp.concatenate([grad_gain_one, grad_gain_two])
    grad_gains = grad_gains.reshape(seq_count, dp_count, gain_part)
    grad_small = jnp.concatenate([grad_biases, grad_gains], axis=-1)
    grad_small = grad_small.reshape(seq_count, dp_count, wide_rows, small_columns)
    late = jnp.concatenate(
        [grad_qkv.reshape(seq_count, dp_count, wide_rows, 3 * width), grad_small], axis=-1
    )
    late = scatter_swaps(late, "dp", dp_count, dp_at, 1)
    late, grad_rows = together(late, grad_rows)
    late = add_up(late).astype(LOW)
    grad_rows = sequence_swap(grad_rows, seq_count, seq_at, sequences)
    grad_tokens = grad_resid_one + grad_rows.reshape(rows, D)
    late = jnp.concatenate([late, grad_out_w], axis=-1)
    late = exchange(late).astype(WIDE)
    small_end = 3 * width + small_columns
    shard_small = jnp.sum(late[:, :, 3 * width : small_end], axis=0).reshape(-1)
    shard_out = jnp.sum(late[:, :, small_end:], axis=0)
    shard_qkv = late[:, :, : 3 * width].reshape(sequences, head_groups, wide_rows, 3, width)
    shard_qkv = jnp.sum(shard_qkv, axis=0).transpose(1, 2, 0, 3)
    shard_qkv = shard_qkv.reshape(wide_rows, 3, padded * HD)[:, :, :D].reshape(wide_rows, 3 * D)

    shape = (sequences, seq_rows, D)
    return (
        layer_out.reshape(shape),
        grad_tokens.reshape(shape),
        shard_qkv,
        shard_out,
        shard_gate_up,
        shard_down,
        shard_small[:bias_part],
        shard_small[bias_part:],
    )


def solution(mesh):
    in_specs = (
        P("dp", "seq", None),
        P("dp", "seq"),
        P("dp", "seq"),
        P(("seq", "dp"), None),
        P(("seq", "dp"), None),
        P(("seq", "dp"), None),
        P(("seq", "dp"), None),
        P(("seq", "dp")),
        P(("seq", "dp")),
        P("dp", "seq", None),
    )
    out_specs = (
        P("dp", "seq", None),
        P("dp", "seq", None),
        P(("seq", "dp"), None),
        P(("seq", "dp"), None),
        P(("seq", "dp"), None),
        P(("seq", "dp"), None),
        P(("seq", "dp")),
        P(("seq", "dp")),
    )

    return jax.shard_map(local, mesh=mesh, in_specs=in_specs, out_specs=out_specs, check_vma=False)
```

```python
import math

import jax
import jax.numpy as jnp
import numpy as np
from jax import lax
from jax.experimental import pallas as pl
from jax.experimental.pallas import tpu as pltpu
from jax.sharding import PartitionSpec as P


D = 768
H = 12
HD = 64
FF = 3072
GROUP = 4
QUERY_BLOCK = 128

NEG_FILL = -1e30
EPSILON = 1e-12
LOW = jnp.bfloat16
WIDE = jnp.float32


def slope_table(head_count):
    nearest = 2 ** int(math.floor(math.log2(head_count)))
    leading = [2.0 ** (-8.0 * (counter + 1) / nearest) for counter in range(nearest)]
    further = [2.0 ** (-8.0 * (counter + 1) / (2 * nearest)) for counter in range(2 * nearest)]
    return np.array(leading + further[0::2][: head_count - nearest], np.float32)


def dot(left, right):
    return jnp.dot(left, right, preferred_element_type=WIDE)


def dot_t(left, right):
    return lax.dot_general(left, right, (((1,), (1,)), ((), ())), preferred_element_type=WIDE)


def dot_w(left, right):
    return lax.dot_general(left, right, (((0,), (0,)), ((), ())), preferred_element_type=WIDE)


def swap(value, axis, size, mask):
    return lax.ppermute(value, axis, [(i, i ^ mask) for i in range(size)])


def put(buffer, value, index, axis):
    starts = [0] * buffer.ndim
    starts[axis] = index
    return lax.dynamic_update_slice(buffer, jnp.expand_dims(value, axis), starts)


def swapped(value, name, size, step=1):
    total = lax.axis_size(name)
    return (value,) + tuple(swap(value, name, total, mask * step) for mask in range(1, size))


def in_order(pieces, place, axis):
    value = pieces[0]
    shape = value.shape[:axis] + (len(pieces),) + value.shape[axis:]
    result = jnp.zeros(shape, value.dtype)
    for mask, piece in enumerate(pieces):
        result = put(result, piece, place ^ mask, axis)
    return result


def gather_by_swaps(value, name, size, place, axis, step=1):
    return in_order(swapped(value, name, size, step), place, axis)


def scatter_swaps(value, name, size, place, axis, step=1):
    total = lax.axis_size(name)
    pieces = [lax.dynamic_index_in_dim(value, place, axis, False)]
    for mask in range(1, size):
        part = lax.dynamic_index_in_dim(value, place ^ mask, axis, False).astype(LOW)
        pieces.append(swap(part, name, total, mask * step))
    return tuple(pieces)


def add_up(pieces):
    result = pieces[0].astype(WIDE)
    for piece in pieces[1:]:
        result = result + piece.astype(WIDE)
    return result


def scatter_by_swaps(value, name, size, place, axis, step=1):
    return add_up(scatter_swaps(value, name, size, place, axis, step))


def group_gather(rows, seq_count):
    partner = swap(rows, "seq", seq_count, 1)
    across = swap(rows, "seq", seq_count, 2)
    corner = swap(across, "seq", seq_count, 1)
    return jnp.concatenate([rows, partner, across, corner], axis=0)


def group_scatter(partial, seq_count):
    rows = partial.shape[0] // GROUP
    blocks = partial.reshape(GROUP, rows, partial.shape[1])
    sent = jnp.stack([blocks[1], blocks[3]]).astype(LOW)
    came = swap(sent, "seq", seq_count, 1).astype(WIDE)
    across = swap((blocks[2] + came[1]).astype(LOW), "seq", seq_count, 2).astype(WIDE)
    return blocks[0] + came[0] + across


def sequence_reduce(blocks, seq_count, seq_at, sequences):
    total, step = blocks, 1
    while total.shape[0] > sequences:
        halves = total.reshape((total.shape[0] // 2, 2) + total.shape[1:])
        bit = (seq_at // step) % 2
        sent = lax.dynamic_index_in_dim(halves, 1 - bit, 1, False).astype(LOW)
        kept = lax.dynamic_index_in_dim(halves, bit, 1, False).astype(WIDE)
        total = kept + swap(sent, "seq", seq_count, step).astype(WIDE)
        step *= 2
    return total


def sequence_swap(total, seq_count, seq_at, sequences):
    step = seq_count // sequences
    own = seq_at // step
    result = put(jnp.zeros_like(total), lax.dynamic_index_in_dim(total, own, 0, False), own, 0)
    for mask in range(1, sequences):
        sent = lax.dynamic_index_in_dim(total, own ^ mask, 0, False).astype(LOW)
        came = swap(sent, "seq", seq_count, mask * step).astype(WIDE)
        result = put(result, came, own ^ mask, 0)
    return result


def head_columns(head, width):
    column = lax.broadcasted_iota(jnp.int32, (1, width), 1)
    return ((column >= head * HD) & (column < (head + 1) * HD)).astype(WIDE).astype(LOW)


def block_scores(query_rows, keys, slope, start, marks_column, marks_row):
    shape = (query_rows.shape[0], keys.shape[0])
    row = lax.broadcasted_iota(jnp.int32, shape, 0) + start
    column = lax.broadcasted_iota(jnp.int32, shape, 1)
    distance = jnp.abs(row - column).astype(WIDE)
    allowed = (marks_column[:, 0:1] == marks_row[0:1]) & (marks_row[1:2] >= marks_column[:, 1:2])
    return jnp.where(allowed, dot_t(query_rows, keys) * 0.125 - slope * distance, NEG_FILL)


def attend_kernel(heads, width, slopes, qkv, marks_column, marks_row, out, sums):
    keys, values = qkv[:, width : 2 * width], qkv[:, 2 * width :]

    def block(index, carry):
        start = pl.multiple_of(index * QUERY_BLOCK, QUERY_BLOCK)
        here = pl.ds(start, QUERY_BLOCK)
        queries, marks = qkv[here, :width], marks_column[here, :]
        blended = jnp.zeros((QUERY_BLOCK, width), WIDE)
        for head in range(heads):
            mask = head_columns(head, width)
            scores = block_scores(queries * mask, keys, slopes[head], start, marks, marks_row[...])
            top_score = jnp.max(scores, axis=-1, keepdims=True)
            exponent = jnp.exp(scores - top_score)
            total = jnp.sum(exponent, axis=-1, keepdims=True)
            blended = blended + dot((exponent / total).astype(LOW), values * mask)
            sums[here, head : head + 1] = top_score + jnp.log(total)
        out[here, :] = blended.astype(LOW)
        return carry

    lax.fori_loop(0, qkv.shape[0] // QUERY_BLOCK, block, 0)


def attend_back_kernel(
    heads, width, slopes, qkv, grad_out, sums, marks_column, marks_row, grad_proj, totals, acc
):
    keys, values = qkv[:, width : 2 * width], qkv[:, 2 * width :]
    acc[...] = jnp.zeros(acc.shape, WIDE)
    totals[...] = jnp.zeros(totals.shape, WIDE)

    def block(index, carry):
        start = pl.multiple_of(index * QUERY_BLOCK, QUERY_BLOCK)
        here = pl.ds(start, QUERY_BLOCK)
        queries, marks, grads = qkv[here, :width], marks_column[here, :], grad_out[here, :]
        grad_query = jnp.zeros((QUERY_BLOCK, width), WIDE)
        grad_key = jnp.zeros((qkv.shape[0], width), WIDE)
        grad_value = jnp.zeros((qkv.shape[0], width), WIDE)
        for head in range(heads):
            mask = head_columns(head, width)
            own_query, own_grad = queries * mask, grads * mask
            scores = block_scores(own_query, keys, slopes[head], start, marks, marks_row[...])
            soft = jnp.exp(scores - sums[here, head : head + 1])
            grad_soft = dot_t(own_grad, values)
            delta = jnp.sum(soft * grad_soft, axis=-1, keepdims=True)
            grad_scores = (soft * (grad_soft - delta)).astype(LOW)
            grad_query = grad_query + dot(grad_scores, keys * mask)
            grad_key = grad_key + dot_w(grad_scores, own_query)
            grad_value = grad_value + dot_w(soft.astype(LOW), own_grad)
        grad_query = grad_query * 0.125
        grad_proj[here, :width] = grad_query.astype(LOW)
        totals[0:1] = totals[0:1] + jnp.sum(grad_query, axis=0, keepdims=True)
        acc[0] = acc[0] + grad_key
        acc[1] = acc[1] + grad_value
        return carry

    lax.fori_loop(0, qkv.shape[0] // QUERY_BLOCK, block, 0)
    grad_proj[:, width : 2 * width] = (acc[0] * 0.125).astype(LOW)
    grad_proj[:, 2 * width :] = acc[1].astype(LOW)
    totals[1:2] = jnp.sum(acc[1], axis=0, keepdims=True)


def attend(heads, width, slopes, qkv, marks_column, marks_row):
    length = qkv.shape[0]
    return pl.pallas_call(
        lambda *refs: attend_kernel(heads, width, *refs),
        out_shape=(
            jax.ShapeDtypeStruct((length, width), LOW),
            jax.ShapeDtypeStruct((length, heads), WIDE),
        ),
        in_specs=[pl.BlockSpec(memory_space=pltpu.SMEM)]
        + [pl.BlockSpec(memory_space=pltpu.VMEM)] * 3,
        out_specs=[pl.BlockSpec(memory_space=pltpu.VMEM)] * 2,
        name="attend",
    )(slopes, qkv, marks_column, marks_row)


def attend_back(heads, width, slopes, qkv, grad_out, sums, marks_column, marks_row):
    length = qkv.shape[0]
    return pl.pallas_call(
        lambda *refs: attend_back_kernel(heads, width, *refs),
        out_shape=(
            jax.ShapeDtypeStruct((length, 3 * width), LOW),
            jax.ShapeDtypeStruct((8, width), WIDE),
        ),
        in_specs=[pl.BlockSpec(memory_space=pltpu.SMEM)]
        + [pl.BlockSpec(memory_space=pltpu.VMEM)] * 5,
        out_specs=[pl.BlockSpec(memory_space=pltpu.VMEM)] * 2,
        scratch_shapes=[pltpu.VMEM((2, length, width), WIDE)],
        name="attend_back",
    )(slopes, qkv, grad_out, sums, marks_column, marks_row)


def norm_forward(resid, norm_gain, norm_bias):
    centre = resid - jnp.mean(resid, axis=-1, keepdims=True)
    inverse = lax.rsqrt(jnp.mean(centre * centre, axis=-1, keepdims=True) + EPSILON)
    normed = centre * inverse
    return (normed * norm_gain + norm_bias, normed, inverse)


def norm_backward(grad_rows, normed, inverse, norm_gain):
    scaled = grad_rows * norm_gain
    first_mean = jnp.mean(scaled, axis=-1, keepdims=True)
    second_mean = jnp.mean(scaled * normed, axis=-1, keepdims=True)
    return inverse * (scaled - first_mean - normed * second_mean)


def geglu(gate_in, up_in):
    return jax.nn.gelu(gate_in, approximate=False) * up_in


def exchange(value):
    return lax.all_to_all(value, "seq", 0, 0)


def together(*values):
    return lax.optimization_barrier(values)


def local(
    tokens, segments, padding, w_qkv, w_out, w_gate_up, w_down, biases, norm_gains, cotangent
):
    sequences, seq_rows = tokens.shape[:2]
    seq_count, dp_count = lax.axis_size("seq"), lax.axis_size("dp")
    seq_at, dp_at = lax.axis_index("seq"), lax.axis_index("dp")
    halves = seq_count // GROUP
    half_at = seq_at // GROUP
    rows = sequences * seq_rows
    length = seq_count * seq_rows
    head_groups = seq_count // sequences
    heads = -(-H // head_groups)
    padded = heads * head_groups
    width = heads * HD
    own_seq, own_heads = seq_at // head_groups, seq_at % head_groups
    wide_rows = w_qkv.shape[0]
    down_rows = w_down.shape[0]
    bias_part, gain_part = biases.shape[0], norm_gains.shape[0]
    run = dp_count * down_rows

    tokens_flat = tokens.reshape(rows, D)

    by_heads = w_qkv.reshape(wide_rows, 3, H, HD)
    by_heads = jnp.pad(by_heads, ((0, 0), (0, 0), (0, padded - H), (0, 0)))
    by_heads = by_heads.reshape(wide_rows, 3, head_groups, width).transpose(2, 0, 1, 3)
    by_heads = by_heads.reshape(1, head_groups, wide_rows, 3 * width)
    by_heads = jnp.broadcast_to(by_heads, (sequences,) + by_heads.shape[1:])
    by_heads = by_heads.reshape(seq_count, wide_rows, 3 * width)
    small_columns = (bias_part + gain_part) // wide_rows
    small = jnp.concatenate([biases, norm_gains]).reshape(1, wide_rows, small_columns)
    small = jnp.broadcast_to(small, (seq_count, wide_rows, small_columns))
    qkv_rows = exchange(jnp.concatenate([by_heads, small], axis=-1))
    qkv_rows, gate_up_in, down_in = together(qkv_rows, w_gate_up, w_down)
    qkv_own = gather_by_swaps(qkv_rows, "dp", dp_count, dp_at, 1)

    marks = jnp.concatenate([segments.reshape(-1), padding.reshape(-1)]).astype(LOW)
    extra_rows = -(-marks.shape[0] // (8 * D)) * 8
    marks = jnp.pad(marks, (0, extra_rows * D - marks.shape[0])).reshape(extra_rows, D)
    packed = jnp.concatenate([tokens_flat, marks], axis=0)
    line = lax.all_gather(packed, "seq", axis=0, tiled=False)
    token_rows = lax.dynamic_slice_in_dim(line[:, :rows], own_seq * seq_rows, seq_rows, 1)
    token_rows = token_rows.reshape(length, D)
    mark_line = line[:, rows:].reshape(seq_count, extra_rows * D)[:, : 2 * rows]
    mark_line = mark_line.reshape(seq_count, 2, sequences, seq_rows)
    mark_line = lax.dynamic_index_in_dim(mark_line, own_seq, 2, False).astype(WIDE)
    marks_row = jnp.stack([mark_line[:, 0].reshape(length), mark_line[:, 1].reshape(length)])
    marks_column = marks_row.T

    out_part = gather_by_swaps(w_out, "dp", dp_count, dp_at, 0).reshape(-1, D)
    out_full = lax.all_gather(out_part, "seq", axis=0, tiled=True)

    columns = gate_up_in.reshape(wide_rows, 2, halves, GROUP, run).transpose(3, 0, 1, 2, 4)
    columns = columns.reshape(1, GROUP, wide_rows, 2 * halves * run)
    columns = jnp.broadcast_to(columns, (halves,) + columns.shape[1:])
    hidden = halves * run
    gate_up_rows = exchange(columns.reshape(seq_count, wide_rows, 2 * hidden))
    gate_up_pieces = swapped(gate_up_rows, "dp", dp_count)
    down_part = gather_by_swaps(down_in, "seq", halves, half_at, 0, GROUP)
    down_pieces = swapped(down_part, "dp", dp_count)

    vectors = qkv_own[..., 3 * width :].reshape(seq_count, dp_count, bias_part + gain_part)
    bias_vector = vectors[:, :, :bias_part].reshape(6 * D).astype(WIDE)
    gain_vector = vectors[:, :, bias_part:].reshape(2 * D).astype(WIDE)
    qkv_own = qkv_own[..., : 3 * width].reshape(D, 3 * width)

    def own_part(vector):
        spread = jnp.pad(vector, (0, padded * HD - D))
        return lax.dynamic_slice_in_dim(spread, own_heads * width, width, 0)

    own_bias = jnp.concatenate(
        [own_part(bias_vector[0:D]), jnp.zeros((width,), WIDE), own_part(bias_vector[D : 2 * D])]
    )
    qkv = (dot(token_rows, qkv_own) + own_bias).astype(LOW)
    slopes = jnp.pad(jnp.asarray(slope_table(H)), (0, padded - H))
    slopes = lax.dynamic_slice_in_dim(slopes, own_heads * heads, heads, 0)
    blended, log_sums = attend(heads, width, slopes, qkv, marks_column, marks_row)
    blended = blended.reshape(seq_count, seq_rows, width)

    def to_rows(by_head):
        arrived = exchange(by_head).reshape(sequences, head_groups, seq_rows, -1, width)
        arrived = arrived.transpose(0, 2, 3, 1, 4).reshape(rows, -1, padded * HD)
        return arrived[:, :, :D].reshape(rows, -1)

    attended = to_rows(blended)
    token_wide = tokens_flat.astype(WIDE)
    resid_one = token_wide + (dot(attended, out_full) + bias_vector[2 * D : 3 * D])
    resid_one, gate_up_pieces, down_pieces = together(resid_one, gate_up_pieces, down_pieces)
    gate_up_own = in_order(gate_up_pieces, dp_at, 1).reshape(D, 2 * hidden)
    down_own = in_order(down_pieces, dp_at, 1).reshape(hidden, D)
    hidden_one, normed_one, inverse_one = norm_forward(
        resid_one, gain_vector[0:D], bias_vector[4 * D : 5 * D]
    )
    hidden_rows = group_gather(hidden_one.astype(LOW), seq_count)
    gate_up = dot(hidden_rows, gate_up_own)
    activated_wide, geglu_back = jax.vjp(geglu, gate_up[:, :hidden], gate_up[:, hidden:])
    activated = activated_wide.astype(LOW)
    mlp_out = group_scatter(dot(activated, down_own), seq_count)
    resid_two = hidden_one + (mlp_out + bias_vector[3 * D : 4 * D])
    normed_out, normed_two, inverse_two = norm_forward(
        resid_two, gain_vector[D : 2 * D], bias_vector[5 * D : 6 * D]
    )
    valid_mask = padding.reshape(rows, 1).astype(WIDE)
    layer_out = (normed_out * valid_mask).astype(LOW)

    grad_final = cotangent.reshape(rows, D).astype(WIDE) * valid_mask
    grad_gain_two = jnp.sum(grad_final * normed_two, axis=0)
    grad_bias_two = jnp.sum(grad_final, axis=0)
    grad_resid_two = norm_backward(grad_final, normed_two, inverse_two, gain_vector[D : 2 * D])
    grad_bias_down = jnp.sum(grad_resid_two, axis=0)
    grad_mlp_rows = group_gather(grad_resid_two.astype(LOW), seq_count)
    grad_activated = dot_t(grad_mlp_rows, down_own)
    grad_gate, grad_up = geglu_back(grad_activated)
    grad_gate_up_low = jnp.concatenate([grad_gate, grad_up], axis=-1).astype(LOW)
    grad_hidden = dot_t(grad_gate_up_low, gate_up_own)
    grad_hidden = grad_resid_two + group_scatter(grad_hidden, seq_count)
    grad_down = dot_w(activated, grad_mlp_rows)
    grad_gate_up = dot_w(hidden_rows, grad_gate_up_low)
    grad_gate_up = grad_gate_up.reshape(seq_count, dp_count, wide_rows, 2 * hidden)
    grad_gate_up = scatter_swaps(grad_gate_up, "dp", dp_count, dp_at, 1)
    shard_down = grad_down.reshape(halves, dp_count, down_rows, D)
    shard_down = scatter_by_swaps(shard_down, "dp", dp_count, dp_at, 1)
    shard_down = scatter_by_swaps(shard_down, "seq", halves, half_at, 0, GROUP)

    grad_gain_one = jnp.sum(grad_hidden * normed_one, axis=0)
    grad_bias_one = jnp.sum(grad_hidden, axis=0)
    grad_resid_one = norm_backward(grad_hidden, normed_one, inverse_one, gain_vector[0:D])
    grad_bias_attn = jnp.sum(grad_resid_one, axis=0)
    grad_attn_low = grad_resid_one.astype(LOW)
    grad_attended = dot_t(grad_attn_low, out_full).astype(LOW)
    grad_out_w = dot_w(attended, grad_attn_low)
    grad_out_w = grad_out_w.reshape(seq_count, dp_count, wide_rows, D)
    grad_out_w = scatter_swaps(grad_out_w, "dp", dp_count, dp_at, 1)

    spread = grad_attended.reshape(sequences, seq_rows, D)
    spread = jnp.pad(spread, ((0, 0), (0, 0), (0, padded * HD - D)))
    spread = spread.reshape(sequences, seq_rows, head_groups, width).transpose(0, 2, 1, 3)
    grad_blended = exchange(spread.reshape(seq_count, seq_rows, width))
    grad_gate_up = add_up(grad_gate_up).astype(LOW)
    grad_blended = grad_blended.reshape(length, width)
    grad_proj, totals = attend_back(
        heads, width, slopes, qkv, grad_blended, log_sums, marks_column, marks_row
    )

    def whole_part(vector):
        spread = jnp.zeros((padded * HD,), WIDE)
        return lax.dynamic_update_slice(spread, vector, (own_heads * width,))[:D]

    grad_bias_query = whole_part(totals[0])
    grad_bias_value = whole_part(totals[1])
    grad_rows = dot_t(grad_proj, qkv_own).astype(LOW).reshape(seq_count, seq_rows, D)
    grad_rows = sequence_reduce(grad_rows, seq_count, seq_at, sequences)
    grad_qkv = dot_w(token_rows, grad_proj)

    early = exchange(grad_gate_up).astype(WIDE)
    shard_gate_up = early.reshape(halves, GROUP, wide_rows, 2 * hidden)
    shard_gate_up = jnp.sum(shard_gate_up, axis=0).reshape(GROUP, wide_rows, 2, halves, run)
    shard_gate_up = shard_gate_up.transpose(1, 2, 3, 0, 4).reshape(wide_rows, 2 * FF)

    grad_biases = jnp.concatenate(
        [
            grad_bias_query,
            grad_bias_value,
            grad_bias_attn,
            grad_bias_down,
            grad_bias_one,
            grad_bias_two,
        ]
    ).reshape(seq_count, dp_count, bias_part)
    grad_gains = jnp.concatenate([grad_gain_one, grad_gain_two])
    grad_gains = grad_gains.reshape(seq_count, dp_count, gain_part)
    grad_small = jnp.concatenate([grad_biases, grad_gains], axis=-1)
    grad_small = grad_small.reshape(seq_count, dp_count, wide_rows, small_columns)
    late = jnp.concatenate(
        [grad_qkv.reshape(seq_count, dp_count, wide_rows, 3 * width), grad_small], axis=-1
    )
    late = scatter_swaps(late, "dp", dp_count, dp_at, 1)
    late, grad_out_w = together(late, grad_out_w)
    late, grad_out_w = add_up(late).astype(LOW), add_up(grad_out_w).astype(LOW)
    grad_rows = sequence_swap(grad_rows, seq_count, seq_at, sequences)
    grad_tokens = grad_resid_one + grad_rows.reshape(rows, D)
    late = jnp.concatenate([late, grad_out_w], axis=-1)
    late = exchange(late).astype(WIDE)
    small_end = 3 * width + small_columns
    shard_small = jnp.sum(late[:, :, 3 * width : small_end], axis=0).reshape(-1)
    shard_out = jnp.sum(late[:, :, small_end:], axis=0)
    shard_qkv = late[:, :, : 3 * width].reshape(sequences, head_groups, wide_rows, 3, width)
    shard_qkv = jnp.sum(shard_qkv, axis=0).transpose(1, 2, 0, 3)
    shard_qkv = shard_qkv.reshape(wide_rows, 3, padded * HD)[:, :, :D].reshape(wide_rows, 3 * D)

    shape = (sequences, seq_rows, D)
    return (
        layer_out.reshape(shape),
        grad_tokens.reshape(shape),
        shard_qkv,
        shard_out,
        shard_gate_up,
        shard_down,
        shard_small[:bias_part],
        shard_small[bias_part:],
    )


def solution(mesh):
    in_specs = (
        P("dp", "seq", None),
        P("dp", "seq"),
        P("dp", "seq"),
        P(("seq", "dp"), None),
        P(("seq", "dp"), None),
        P(("seq", "dp"), None),
        P(("seq", "dp"), None),
        P(("seq", "dp")),
        P(("seq", "dp")),
        P("dp", "seq", None),
    )
    out_specs = (
        P("dp", "seq", None),
        P("dp", "seq", None),
        P(("seq", "dp"), None),
        P(("seq", "dp"), None),
        P(("seq", "dp"), None),
        P(("seq", "dp"), None),
        P(("seq", "dp")),
        P(("seq", "dp")),
    )

    return jax.shard_map(local, mesh=mesh, in_specs=in_specs, out_specs=out_specs, check_vma=False)
```

```python
import math

import jax
import jax.numpy as jnp
import numpy as np
from jax import lax
from jax.experimental import pallas as pl
from jax.experimental.pallas import tpu as pltpu
from jax.sharding import PartitionSpec as P


D = 768
H = 12
HD = 64
FF = 3072
GROUP = 4
QUERY_BLOCK = 128

NEG_FILL = -1e30
EPSILON = 1e-12
LOW = jnp.bfloat16
WIDE = jnp.float32


def slope_table(head_count):
    nearest = 2 ** int(math.floor(math.log2(head_count)))
    leading = [2.0 ** (-8.0 * (counter + 1) / nearest) for counter in range(nearest)]
    further = [2.0 ** (-8.0 * (counter + 1) / (2 * nearest)) for counter in range(2 * nearest)]
    return np.array(leading + further[0::2][: head_count - nearest], np.float32)


def dot(left, right):
    return jnp.dot(left, right, preferred_element_type=WIDE)


def dot_t(left, right):
    return lax.dot_general(left, right, (((1,), (1,)), ((), ())), preferred_element_type=WIDE)


def dot_w(left, right):
    return lax.dot_general(left, right, (((0,), (0,)), ((), ())), preferred_element_type=WIDE)


def swap(value, axis, size, mask):
    return lax.ppermute(value, axis, [(i, i ^ mask) for i in range(size)])


def put(buffer, value, index, axis):
    starts = [0] * buffer.ndim
    starts[axis] = index
    return lax.dynamic_update_slice(buffer, jnp.expand_dims(value, axis), starts)


def swapped(value, name, size, step=1):
    total = lax.axis_size(name)
    return (value,) + tuple(swap(value, name, total, mask * step) for mask in range(1, size))


def in_order(pieces, place, axis):
    value = pieces[0]
    shape = value.shape[:axis] + (len(pieces),) + value.shape[axis:]
    result = jnp.zeros(shape, value.dtype)
    for mask, piece in enumerate(pieces):
        result = put(result, piece, place ^ mask, axis)
    return result


def gather_by_swaps(value, name, size, place, axis, step=1):
    return in_order(swapped(value, name, size, step), place, axis)


def scatter_swaps(value, name, size, place, axis, step=1):
    total = lax.axis_size(name)
    pieces = [lax.dynamic_index_in_dim(value, place, axis, False)]
    for mask in range(1, size):
        part = lax.dynamic_index_in_dim(value, place ^ mask, axis, False).astype(LOW)
        pieces.append(swap(part, name, total, mask * step))
    return tuple(pieces)


def add_up(pieces):
    result = pieces[0].astype(WIDE)
    for piece in pieces[1:]:
        result = result + piece.astype(WIDE)
    return result


def scatter_by_swaps(value, name, size, place, axis, step=1):
    return add_up(scatter_swaps(value, name, size, place, axis, step))


def group_gather(rows, seq_count):
    partner = swap(rows, "seq", seq_count, 1)
    across = swap(rows, "seq", seq_count, 2)
    corner = swap(across, "seq", seq_count, 1)
    return jnp.concatenate([rows, partner, across, corner], axis=0)


def group_scatter(kept, sent, seq_count):
    came = swap(sent, "seq", seq_count, 1).astype(WIDE)
    across = swap((kept[1] + came[1]).astype(LOW), "seq", seq_count, 2).astype(WIDE)
    return kept[0] + came[0] + across


def sequence_reduce(blocks, seq_count, seq_at, sequences):
    total, step = blocks, 1
    while total.shape[0] > sequences:
        halves = total.reshape((total.shape[0] // 2, 2) + total.shape[1:])
        bit = (seq_at // step) % 2
        sent = lax.dynamic_index_in_dim(halves, 1 - bit, 1, False).astype(LOW)
        kept = lax.dynamic_index_in_dim(halves, bit, 1, False).astype(WIDE)
        total = kept + swap(sent, "seq", seq_count, step).astype(WIDE)
        step *= 2
    return total


def sequence_swap(total, seq_count, seq_at, sequences):
    step = seq_count // sequences
    own = seq_at // step
    result = put(jnp.zeros_like(total), lax.dynamic_index_in_dim(total, own, 0, False), own, 0)
    for mask in range(1, sequences):
        sent = lax.dynamic_index_in_dim(total, own ^ mask, 0, False).astype(LOW)
        came = swap(sent, "seq", seq_count, mask * step).astype(WIDE)
        result = put(result, came, own ^ mask, 0)
    return result


def head_columns(head, width):
    column = lax.broadcasted_iota(jnp.int32, (1, width), 1)
    return ((column >= head * HD) & (column < (head + 1) * HD)).astype(WIDE).astype(LOW)


def block_scores(query_rows, keys, slope, start, marks_column, marks_row):
    shape = (query_rows.shape[0], keys.shape[0])
    row = lax.broadcasted_iota(jnp.int32, shape, 0) + start
    column = lax.broadcasted_iota(jnp.int32, shape, 1)
    distance = jnp.abs(row - column).astype(WIDE)
    allowed = (marks_column[:, 0:1] == marks_row[0:1]) & (marks_row[1:2] >= marks_column[:, 1:2])
    return jnp.where(allowed, dot_t(query_rows, keys) * 0.125 - slope * distance, NEG_FILL)


def attend_kernel(heads, width, slopes, qkv, marks_column, marks_row, out, sums):
    keys, values = qkv[:, width : 2 * width], qkv[:, 2 * width :]

    def block(index, carry):
        start = pl.multiple_of(index * QUERY_BLOCK, QUERY_BLOCK)
        here = pl.ds(start, QUERY_BLOCK)
        queries, marks = qkv[here, :width], marks_column[here, :]
        blended = jnp.zeros((QUERY_BLOCK, width), WIDE)
        for head in range(heads):
            mask = head_columns(head, width)
            scores = block_scores(queries * mask, keys, slopes[head], start, marks, marks_row[...])
            top_score = jnp.max(scores, axis=-1, keepdims=True)
            exponent = jnp.exp(scores - top_score)
            total = jnp.sum(exponent, axis=-1, keepdims=True)
            blended = blended + dot((exponent / total).astype(LOW), values * mask)
            sums[here, head : head + 1] = top_score + jnp.log(total)
        out[here, :] = blended.astype(LOW)
        return carry

    lax.fori_loop(0, qkv.shape[0] // QUERY_BLOCK, block, 0)


def attend_back_kernel(
    heads, width, slopes, qkv, grad_out, sums, marks_column, marks_row, grad_proj, totals, acc
):
    keys, values = qkv[:, width : 2 * width], qkv[:, 2 * width :]
    acc[...] = jnp.zeros(acc.shape, WIDE)
    totals[...] = jnp.zeros(totals.shape, WIDE)

    def block(index, carry):
        start = pl.multiple_of(index * QUERY_BLOCK, QUERY_BLOCK)
        here = pl.ds(start, QUERY_BLOCK)
        queries, marks, grads = qkv[here, :width], marks_column[here, :], grad_out[here, :]
        grad_query = jnp.zeros((QUERY_BLOCK, width), WIDE)
        grad_key = jnp.zeros((qkv.shape[0], width), WIDE)
        grad_value = jnp.zeros((qkv.shape[0], width), WIDE)
        for head in range(heads):
            mask = head_columns(head, width)
            own_query, own_grad = queries * mask, grads * mask
            scores = block_scores(own_query, keys, slopes[head], start, marks, marks_row[...])
            soft = jnp.exp(scores - sums[here, head : head + 1])
            grad_soft = dot_t(own_grad, values)
            delta = jnp.sum(soft * grad_soft, axis=-1, keepdims=True)
            grad_scores = (soft * (grad_soft - delta)).astype(LOW)
            grad_query = grad_query + dot(grad_scores, keys * mask)
            grad_key = grad_key + dot_w(grad_scores, own_query)
            grad_value = grad_value + dot_w(soft.astype(LOW), own_grad)
        grad_query = grad_query * 0.125
        grad_proj[here, :width] = grad_query.astype(LOW)
        totals[0:1] = totals[0:1] + jnp.sum(grad_query, axis=0, keepdims=True)
        acc[0] = acc[0] + grad_key
        acc[1] = acc[1] + grad_value
        return carry

    lax.fori_loop(0, qkv.shape[0] // QUERY_BLOCK, block, 0)
    grad_proj[:, width : 2 * width] = (acc[0] * 0.125).astype(LOW)
    grad_proj[:, 2 * width :] = acc[1].astype(LOW)
    totals[1:2] = jnp.sum(acc[1], axis=0, keepdims=True)


def attend(heads, width, slopes, qkv, marks_column, marks_row):
    length = qkv.shape[0]
    return pl.pallas_call(
        lambda *refs: attend_kernel(heads, width, *refs),
        out_shape=(
            jax.ShapeDtypeStruct((length, width), LOW),
            jax.ShapeDtypeStruct((length, heads), WIDE),
        ),
        in_specs=[pl.BlockSpec(memory_space=pltpu.SMEM)]
        + [pl.BlockSpec(memory_space=pltpu.VMEM)] * 3,
        out_specs=[pl.BlockSpec(memory_space=pltpu.VMEM)] * 2,
        name="attend",
    )(slopes, qkv, marks_column, marks_row)


def attend_back(heads, width, slopes, qkv, grad_out, sums, marks_column, marks_row):
    length = qkv.shape[0]
    return pl.pallas_call(
        lambda *refs: attend_back_kernel(heads, width, *refs),
        out_shape=(
            jax.ShapeDtypeStruct((length, 3 * width), LOW),
            jax.ShapeDtypeStruct((8, width), WIDE),
        ),
        in_specs=[pl.BlockSpec(memory_space=pltpu.SMEM)]
        + [pl.BlockSpec(memory_space=pltpu.VMEM)] * 5,
        out_specs=[pl.BlockSpec(memory_space=pltpu.VMEM)] * 2,
        scratch_shapes=[pltpu.VMEM((2, length, width), WIDE)],
        name="attend_back",
    )(slopes, qkv, grad_out, sums, marks_column, marks_row)


def norm_forward(resid, norm_gain, norm_bias):
    centre = resid - jnp.mean(resid, axis=-1, keepdims=True)
    inverse = lax.rsqrt(jnp.mean(centre * centre, axis=-1, keepdims=True) + EPSILON)
    normed = centre * inverse
    return (normed * norm_gain + norm_bias, normed, inverse)


def norm_backward(grad_rows, normed, inverse, norm_gain):
    scaled = grad_rows * norm_gain
    first_mean = jnp.mean(scaled, axis=-1, keepdims=True)
    second_mean = jnp.mean(scaled * normed, axis=-1, keepdims=True)
    return inverse * (scaled - first_mean - normed * second_mean)


def split_store(kept, sent, block, value):
    if block % 2:
        sent[block // 2] = value.astype(LOW)
    else:
        kept[block // 2] = value


def mlp_kernel(hidden, rows, gate_up_own, down_own, kept, sent, activated, through_gate, through_up):
    for block in range(GROUP):
        here = pl.ds(block * (rows.shape[0] // GROUP), rows.shape[0] // GROUP)
        gate_up = dot(rows[here, :], gate_up_own[...])
        gate, up = gate_up[:, :hidden], gate_up[:, hidden:]
        below = 0.5 * (1.0 + lax.erf(gate * math.sqrt(0.5)))
        density = jnp.exp(-0.5 * gate * gate) * (1.0 / math.sqrt(2.0 * math.pi))
        gelu = gate * below
        low = (gelu * up).astype(LOW)
        activated[here, :] = low
        through_gate[here, :] = up * (below + gate * density)
        through_up[here, :] = gelu
        split_store(kept, sent, block, dot(low, down_own[...]))


def mlp_back_kernel(
    hidden, grads, through_gate, through_up, gate_up_own, down_own, kept, sent, grad_gate_up
):
    grad_activated = dot_t(grads[...], down_own[...])
    grad_gate_up[:, :hidden] = (grad_activated * through_gate[...]).astype(LOW)
    grad_gate_up[:, hidden:] = (grad_activated * through_up[...]).astype(LOW)
    partial = dot_t(grad_gate_up[...], gate_up_own[...])
    count = grads.shape[0] // GROUP
    for block in range(GROUP):
        split_store(kept, sent, block, partial[block * count : (block + 1) * count])


def in_vmem(kernel, out_shape, *arrays):
    return pl.pallas_call(
        kernel,
        out_shape=out_shape,
        in_specs=[pl.BlockSpec(memory_space=pltpu.VMEM)] * len(arrays),
        out_specs=jax.tree.map(lambda _: pl.BlockSpec(memory_space=pltpu.VMEM), out_shape),
    )(*arrays)


def split_shapes(count):
    half = (GROUP // 2, count // GROUP, D)
    return jax.ShapeDtypeStruct(half, WIDE), jax.ShapeDtypeStruct(half, LOW)


def mlp_forward(rows, gate_up_own, down_own):
    count, hidden = rows.shape[0], down_own.shape[0]
    out_shape = split_shapes(count) + (
        jax.ShapeDtypeStruct((count, hidden), LOW),
        jax.ShapeDtypeStruct((count, hidden), WIDE),
        jax.ShapeDtypeStruct((count, hidden), WIDE),
    )
    kernel = lambda *refs: mlp_kernel(hidden, *refs)
    return in_vmem(kernel, out_shape, rows, gate_up_own, down_own)


def mlp_backward(grads, through_gate, through_up, gate_up_own, down_own):
    count, hidden = grads.shape[0], down_own.shape[0]
    out_shape = split_shapes(count) + (jax.ShapeDtypeStruct((count, 2 * hidden), LOW),)
    kernel = lambda *refs: mlp_back_kernel(hidden, *refs)
    arrays = (grads, through_gate, through_up, gate_up_own, down_own)
    return in_vmem(kernel, out_shape, *arrays)


def exchange(value):
    return lax.all_to_all(value, "seq", 0, 0)


def together(*values):
    return lax.optimization_barrier(values)


def local(
    tokens, segments, padding, w_qkv, w_out, w_gate_up, w_down, biases, norm_gains, cotangent
):
    sequences, seq_rows = tokens.shape[:2]
    seq_count, dp_count = lax.axis_size("seq"), lax.axis_size("dp")
    seq_at, dp_at = lax.axis_index("seq"), lax.axis_index("dp")
    halves = seq_count // GROUP
    half_at = seq_at // GROUP
    rows = sequences * seq_rows
    length = seq_count * seq_rows
    head_groups = seq_count // sequences
    heads = -(-H // head_groups)
    padded = heads * head_groups
    width = heads * HD
    own_seq, own_heads = seq_at // head_groups, seq_at % head_groups
    wide_rows = w_qkv.shape[0]
    down_rows = w_down.shape[0]
    bias_part, gain_part = biases.shape[0], norm_gains.shape[0]
    run = dp_count * down_rows

    tokens_flat = tokens.reshape(rows, D)

    by_heads = w_qkv.reshape(wide_rows, 3, H, HD)
    by_heads = jnp.pad(by_heads, ((0, 0), (0, 0), (0, padded - H), (0, 0)))
    by_heads = by_heads.reshape(wide_rows, 3, head_groups, width).transpose(2, 0, 1, 3)
    by_heads = by_heads.reshape(1, head_groups, wide_rows, 3 * width)
    by_heads = jnp.broadcast_to(by_heads, (sequences,) + by_heads.shape[1:])
    by_heads = by_heads.reshape(seq_count, wide_rows, 3 * width)
    small_columns = (bias_part + gain_part) // wide_rows
    small = jnp.concatenate([biases, norm_gains]).reshape(1, wide_rows, small_columns)
    small = jnp.broadcast_to(small, (seq_count, wide_rows, small_columns))
    qkv_rows = exchange(jnp.concatenate([by_heads, small], axis=-1))
    qkv_rows, gate_up_in, down_in = together(qkv_rows, w_gate_up, w_down)
    qkv_own = gather_by_swaps(qkv_rows, "dp", dp_count, dp_at, 1)

    marks = jnp.concatenate([segments.reshape(-1), padding.reshape(-1)]).astype(LOW)
    extra_rows = -(-marks.shape[0] // (8 * D)) * 8
    marks = jnp.pad(marks, (0, extra_rows * D - marks.shape[0])).reshape(extra_rows, D)
    packed = jnp.concatenate([tokens_flat, marks], axis=0)
    line = lax.all_gather(packed, "seq", axis=0, tiled=False)
    token_rows = lax.dynamic_slice_in_dim(line[:, :rows], own_seq * seq_rows, seq_rows, 1)
    token_rows = token_rows.reshape(length, D)
    mark_line = line[:, rows:].reshape(seq_count, extra_rows * D)[:, : 2 * rows]
    mark_line = mark_line.reshape(seq_count, 2, sequences, seq_rows)
    mark_line = lax.dynamic_index_in_dim(mark_line, own_seq, 2, False).astype(WIDE)
    marks_row = jnp.stack([mark_line[:, 0].reshape(length), mark_line[:, 1].reshape(length)])
    marks_column = marks_row.T

    out_part = gather_by_swaps(w_out, "dp", dp_count, dp_at, 0).reshape(-1, D)
    out_full = lax.all_gather(out_part, "seq", axis=0, tiled=True)

    columns = gate_up_in.reshape(wide_rows, 2, halves, GROUP, run).transpose(3, 0, 1, 2, 4)
    columns = columns.reshape(1, GROUP, wide_rows, 2 * halves * run)
    columns = jnp.broadcast_to(columns, (halves,) + columns.shape[1:])
    hidden = halves * run
    gate_up_rows = exchange(columns.reshape(seq_count, wide_rows, 2 * hidden))
    gate_up_pieces = swapped(gate_up_rows, "dp", dp_count)
    down_part = gather_by_swaps(down_in, "seq", halves, half_at, 0, GROUP)
    down_pieces = swapped(down_part, "dp", dp_count)

    vectors = qkv_own[..., 3 * width :].reshape(seq_count, dp_count, bias_part + gain_part)
    bias_vector = vectors[:, :, :bias_part].reshape(6 * D).astype(WIDE)
    gain_vector = vectors[:, :, bias_part:].reshape(2 * D).astype(WIDE)
    qkv_own = qkv_own[..., : 3 * width].reshape(D, 3 * width)

    def own_part(vector):
        spread = jnp.pad(vector, (0, padded * HD - D))
        return lax.dynamic_slice_in_dim(spread, own_heads * width, width, 0)

    own_bias = jnp.concatenate(
        [own_part(bias_vector[0:D]), jnp.zeros((width,), WIDE), own_part(bias_vector[D : 2 * D])]
    )
    qkv = (dot(token_rows, qkv_own) + own_bias).astype(LOW)
    slopes = jnp.pad(jnp.asarray(slope_table(H)), (0, padded - H))
    slopes = lax.dynamic_slice_in_dim(slopes, own_heads * heads, heads, 0)
    blended, log_sums = attend(heads, width, slopes, qkv, marks_column, marks_row)
    blended = blended.reshape(seq_count, seq_rows, width)

    def to_rows(by_head):
        arrived = exchange(by_head).reshape(sequences, head_groups, seq_rows, -1, width)
        arrived = arrived.transpose(0, 2, 3, 1, 4).reshape(rows, -1, padded * HD)
        return arrived[:, :, :D].reshape(rows, -1)

    attended = to_rows(blended)
    attended, bias_parts, gain_parts = together(
        attended, jnp.split(bias_vector, 6), jnp.split(gain_vector, 2)
    )
    token_wide = tokens_flat.astype(WIDE)
    resid_one = token_wide + (dot(attended, out_full) + bias_parts[2])
    resid_one, gate_up_pieces, down_pieces = together(resid_one, gate_up_pieces, down_pieces)
    gate_up_own = in_order(gate_up_pieces, dp_at, 1).reshape(D, 2 * hidden)
    down_own = in_order(down_pieces, dp_at, 1).reshape(hidden, D)
    hidden_one, normed_one, inverse_one = norm_forward(
        resid_one, gain_parts[0], bias_parts[4]
    )
    hidden_rows = group_gather(hidden_one.astype(LOW), seq_count)
    kept, sent, activated, through_gate, through_up = mlp_forward(
        hidden_rows, gate_up_own, down_own
    )
    mlp_out = group_scatter(kept, sent, seq_count)
    resid_two = hidden_one + (mlp_out + bias_parts[3])
    normed_out, normed_two, inverse_two = norm_forward(
        resid_two, gain_parts[1], bias_parts[5]
    )
    valid_mask = padding.reshape(rows, 1).astype(WIDE)
    layer_out = (normed_out * valid_mask).astype(LOW)

    grad_final = cotangent.reshape(rows, D).astype(WIDE) * valid_mask
    grad_gain_two = jnp.sum(grad_final * normed_two, axis=0)
    grad_bias_two = jnp.sum(grad_final, axis=0)
    grad_resid_two = norm_backward(grad_final, normed_two, inverse_two, gain_parts[1])
    grad_bias_down = jnp.sum(grad_resid_two, axis=0)
    grad_mlp_rows = group_gather(grad_resid_two.astype(LOW), seq_count)
    kept, sent, grad_gate_up_low = mlp_backward(
        grad_mlp_rows, through_gate, through_up, gate_up_own, down_own
    )
    grad_hidden = grad_resid_two + group_scatter(kept, sent, seq_count)
    grad_down = dot_w(activated, grad_mlp_rows)
    grad_gate_up = dot_w(hidden_rows, grad_gate_up_low)
    grad_gate_up = grad_gate_up.reshape(seq_count, dp_count, wide_rows, 2 * hidden)
    grad_gate_up = scatter_swaps(grad_gate_up, "dp", dp_count, dp_at, 1)
    shard_down = grad_down.reshape(halves, dp_count, down_rows, D)
    shard_down = scatter_by_swaps(shard_down, "dp", dp_count, dp_at, 1)
    shard_down = scatter_by_swaps(shard_down, "seq", halves, half_at, 0, GROUP)

    grad_gain_one = jnp.sum(grad_hidden * normed_one, axis=0)
    grad_bias_one = jnp.sum(grad_hidden, axis=0)
    grad_resid_one = norm_backward(grad_hidden, normed_one, inverse_one, gain_parts[0])
    grad_bias_attn = jnp.sum(grad_resid_one, axis=0)
    grad_attn_low = grad_resid_one.astype(LOW)
    grad_attended = dot_t(grad_attn_low, out_full).astype(LOW)
    grad_out_w = dot_w(attended, grad_attn_low)
    grad_out_w = grad_out_w.reshape(seq_count, dp_count, wide_rows, D)
    grad_out_w = scatter_swaps(grad_out_w, "dp", dp_count, dp_at, 1)

    spread = grad_attended.reshape(sequences, seq_rows, D)
    spread = jnp.pad(spread, ((0, 0), (0, 0), (0, padded * HD - D)))
    spread = spread.reshape(sequences, seq_rows, head_groups, width).transpose(0, 2, 1, 3)
    grad_blended = exchange(spread.reshape(seq_count, seq_rows, width))
    grad_gate_up = add_up(grad_gate_up).astype(LOW)
    grad_blended = grad_blended.reshape(length, width)
    grad_proj, totals = attend_back(
        heads, width, slopes, qkv, grad_blended, log_sums, marks_column, marks_row
    )

    def whole_part(vector):
        spread = jnp.zeros((padded * HD,), WIDE)
        return lax.dynamic_update_slice(spread, vector, (own_heads * width,))[:D]

    grad_bias_query = whole_part(totals[0])
    grad_bias_value = whole_part(totals[1])
    grad_rows = dot_t(grad_proj, qkv_own).astype(LOW).reshape(seq_count, seq_rows, D)
    grad_rows = sequence_reduce(grad_rows, seq_count, seq_at, sequences)
    grad_qkv = dot_w(token_rows, grad_proj)

    early = exchange(grad_gate_up).astype(WIDE)
    shard_gate_up = early.reshape(halves, GROUP, wide_rows, 2 * hidden)
    shard_gate_up = jnp.sum(shard_gate_up, axis=0).reshape(GROUP, wide_rows, 2, halves, run)
    shard_gate_up = shard_gate_up.transpose(1, 2, 3, 0, 4).reshape(wide_rows, 2 * FF)

    grad_biases = jnp.concatenate(
        [
            grad_bias_query,
            grad_bias_value,
            grad_bias_attn,
            grad_bias_down,
            grad_bias_one,
            grad_bias_two,
        ]
    ).astype(LOW).reshape(seq_count, dp_count, bias_part)
    grad_gains = jnp.concatenate([grad_gain_one, grad_gain_two]).astype(LOW)
    grad_gains = grad_gains.reshape(seq_count, dp_count, gain_part)
    grad_small = jnp.concatenate([grad_biases, grad_gains], axis=-1)
    grad_small = grad_small.reshape(seq_count, dp_count, wide_rows, small_columns)
    late = jnp.concatenate(
        [grad_qkv.reshape(seq_count, dp_count, wide_rows, 3 * width), grad_small], axis=-1
    )
    late = scatter_swaps(late, "dp", dp_count, dp_at, 1)
    late, grad_out_w = together(late, grad_out_w)
    late, grad_out_w = add_up(late).astype(LOW), add_up(grad_out_w).astype(LOW)
    grad_rows = sequence_swap(grad_rows, seq_count, seq_at, sequences)
    grad_tokens = grad_resid_one + grad_rows.reshape(rows, D)
    late = jnp.concatenate([late, grad_out_w], axis=-1)
    late = exchange(late).astype(WIDE)
    small_end = 3 * width + small_columns
    shard_small = jnp.sum(late[:, :, 3 * width : small_end], axis=0).reshape(-1)
    shard_out = jnp.sum(late[:, :, small_end:], axis=0)
    shard_qkv = late[:, :, : 3 * width].reshape(sequences, head_groups, wide_rows, 3, width)
    shard_qkv = jnp.sum(shard_qkv, axis=0).transpose(1, 2, 0, 3)
    shard_qkv = shard_qkv.reshape(wide_rows, 3, padded * HD)[:, :, :D].reshape(wide_rows, 3 * D)

    shape = (sequences, seq_rows, D)
    return (
        layer_out.reshape(shape),
        grad_tokens.reshape(shape),
        shard_qkv,
        shard_out,
        shard_gate_up,
        shard_down,
        shard_small[:bias_part],
        shard_small[bias_part:],
    )


def solution(mesh):
    in_specs = (
        P("dp", "seq", None),
        P("dp", "seq"),
        P("dp", "seq"),
        P(("seq", "dp"), None),
        P(("seq", "dp"), None),
        P(("seq", "dp"), None),
        P(("seq", "dp"), None),
        P(("seq", "dp")),
        P(("seq", "dp")),
        P("dp", "seq", None),
    )
    out_specs = (
        P("dp", "seq", None),
        P("dp", "seq", None),
        P(("seq", "dp"), None),
        P(("seq", "dp"), None),
        P(("seq", "dp"), None),
        P(("seq", "dp"), None),
        P(("seq", "dp")),
        P(("seq", "dp")),
    )

    return jax.shard_map(local, mesh=mesh, in_specs=in_specs, out_specs=out_specs, check_vma=False)
```

```python
import math

import jax
import jax.numpy as jnp
import numpy as np
from jax import lax
from jax.experimental import pallas as pl
from jax.experimental.pallas import tpu as pltpu
from jax.sharding import PartitionSpec as P


D = 768
H = 12
HD = 64
FF = 3072
GROUP = 4
QUERY_BLOCK = 128

NEG_FILL = -1e30
EPSILON = 1e-12
LOW = jnp.bfloat16
WIDE = jnp.float32


def slope_table(head_count):
    nearest = 2 ** int(math.floor(math.log2(head_count)))
    leading = [2.0 ** (-8.0 * (counter + 1) / nearest) for counter in range(nearest)]
    further = [2.0 ** (-8.0 * (counter + 1) / (2 * nearest)) for counter in range(2 * nearest)]
    return np.array(leading + further[0::2][: head_count - nearest], np.float32)


def dot(left, right):
    return jnp.dot(left, right, preferred_element_type=WIDE)


def dot_t(left, right):
    return lax.dot_general(left, right, (((1,), (1,)), ((), ())), preferred_element_type=WIDE)


def dot_w(left, right):
    return lax.dot_general(left, right, (((0,), (0,)), ((), ())), preferred_element_type=WIDE)


def swap(value, axis, size, mask):
    return lax.ppermute(value, axis, [(i, i ^ mask) for i in range(size)])


def put(buffer, value, index, axis):
    starts = [0] * buffer.ndim
    starts[axis] = index
    return lax.dynamic_update_slice(buffer, jnp.expand_dims(value, axis), starts)


def swapped(value, name, size, step=1):
    total = lax.axis_size(name)
    return (value,) + tuple(swap(value, name, total, mask * step) for mask in range(1, size))


def in_order(pieces, place, axis):
    value = pieces[0]
    shape = value.shape[:axis] + (len(pieces),) + value.shape[axis:]
    result = jnp.zeros(shape, value.dtype)
    for mask, piece in enumerate(pieces):
        result = put(result, piece, place ^ mask, axis)
    return result


def gather_by_swaps(value, name, size, place, axis, step=1):
    return in_order(swapped(value, name, size, step), place, axis)


def scatter_swaps(value, name, size, place, axis, step=1):
    total = lax.axis_size(name)
    pieces = [lax.dynamic_index_in_dim(value, place, axis, False)]
    for mask in range(1, size):
        part = lax.dynamic_index_in_dim(value, place ^ mask, axis, False).astype(LOW)
        pieces.append(swap(part, name, total, mask * step))
    return tuple(pieces)


def line_gather(blocks, reach, seq_count, seq_at):
    while reach:
        came = swap(blocks, "seq", seq_count, reach)
        upper = (seq_at // reach) % 2 == 1
        pair = (jnp.where(upper, came, blocks), jnp.where(upper, blocks, came))
        blocks = jnp.stack(pair, axis=1).reshape((2 * blocks.shape[0],) + blocks.shape[1:])
        reach = reach // 2
    return blocks


def add_up(pieces):
    result = pieces[0].astype(WIDE)
    for piece in pieces[1:]:
        result = result + piece.astype(WIDE)
    return result


def scatter_by_swaps(value, name, size, place, axis, step=1):
    return add_up(scatter_swaps(value, name, size, place, axis, step))


def group_gather(rows, seq_count):
    partner = swap(rows, "seq", seq_count, 1)
    across = swap(rows, "seq", seq_count, 2)
    corner = swap(across, "seq", seq_count, 1)
    return jnp.concatenate([rows, partner, across, corner], axis=0)


def group_scatter(kept, sent, seq_count):
    came = swap(sent, "seq", seq_count, 1).astype(WIDE)
    across = swap((kept[1] + came[1]).astype(LOW), "seq", seq_count, 2).astype(WIDE)
    return kept[0] + came[0] + across


def sequence_reduce(blocks, seq_count, seq_at, sequences):
    total, step = blocks, 1
    while total.shape[0] > sequences:
        halves = total.reshape((total.shape[0] // 2, 2) + total.shape[1:])
        bit = (seq_at // step) % 2
        sent = lax.dynamic_index_in_dim(halves, 1 - bit, 1, False).astype(LOW)
        kept = lax.dynamic_index_in_dim(halves, bit, 1, False).astype(WIDE)
        total = kept + swap(sent, "seq", seq_count, step).astype(WIDE)
        step *= 2
    return total


def sequence_swap(total, seq_count, seq_at, sequences):
    step = seq_count // sequences
    own = seq_at // step
    result = put(jnp.zeros_like(total), lax.dynamic_index_in_dim(total, own, 0, False), own, 0)
    for mask in range(1, sequences):
        sent = lax.dynamic_index_in_dim(total, own ^ mask, 0, False).astype(LOW)
        came = swap(sent, "seq", seq_count, mask * step).astype(WIDE)
        result = put(result, came, own ^ mask, 0)
    return result


def head_columns(head, width):
    column = lax.broadcasted_iota(jnp.int32, (1, width), 1)
    return ((column >= head * HD) & (column < (head + 1) * HD)).astype(WIDE).astype(LOW)


def block_scores(query_rows, keys, slope, start, marks_column, marks_row):
    shape = (query_rows.shape[0], keys.shape[0])
    row = lax.broadcasted_iota(jnp.int32, shape, 0) + start
    column = lax.broadcasted_iota(jnp.int32, shape, 1)
    distance = jnp.abs(row - column).astype(WIDE)
    allowed = (marks_column[:, 0:1] == marks_row[0:1]) & (marks_row[1:2] >= marks_column[:, 1:2])
    return jnp.where(allowed, dot_t(query_rows, keys) * 0.125 - slope * distance, NEG_FILL)


def attend_kernel(heads, width, slopes, qkv, marks_column, marks_row, out, sums):
    keys, values = qkv[:, width : 2 * width], qkv[:, 2 * width :]

    def block(index, carry):
        start = pl.multiple_of(index * QUERY_BLOCK, QUERY_BLOCK)
        here = pl.ds(start, QUERY_BLOCK)
        queries, marks = qkv[here, :width], marks_column[here, :]
        blended = jnp.zeros((QUERY_BLOCK, width), WIDE)
        for head in range(heads):
            mask = head_columns(head, width)
            scores = block_scores(queries * mask, keys, slopes[head], start, marks, marks_row[...])
            top_score = jnp.max(scores, axis=-1, keepdims=True)
            exponent = jnp.exp(scores - top_score)
            total = jnp.sum(exponent, axis=-1, keepdims=True)
            blended = blended + dot((exponent / total).astype(LOW), values * mask)
            sums[here, head : head + 1] = top_score + jnp.log(total)
        out[here, :] = blended.astype(LOW)
        return carry

    lax.fori_loop(0, qkv.shape[0] // QUERY_BLOCK, block, 0)


def attend_back_kernel(
    heads, width, slopes, qkv, grad_out, sums, marks_column, marks_row, grad_proj, totals, acc
):
    keys, values = qkv[:, width : 2 * width], qkv[:, 2 * width :]
    acc[...] = jnp.zeros(acc.shape, WIDE)
    totals[...] = jnp.zeros(totals.shape, WIDE)

    def block(index, carry):
        start = pl.multiple_of(index * QUERY_BLOCK, QUERY_BLOCK)
        here = pl.ds(start, QUERY_BLOCK)
        queries, marks, grads = qkv[here, :width], marks_column[here, :], grad_out[here, :]
        grad_query = jnp.zeros((QUERY_BLOCK, width), WIDE)
        grad_key = jnp.zeros((qkv.shape[0], width), WIDE)
        grad_value = jnp.zeros((qkv.shape[0], width), WIDE)
        for head in range(heads):
            mask = head_columns(head, width)
            own_query, own_grad = queries * mask, grads * mask
            scores = block_scores(own_query, keys, slopes[head], start, marks, marks_row[...])
            soft = jnp.exp(scores - sums[here, head : head + 1])
            grad_soft = dot_t(own_grad, values)
            delta = jnp.sum(soft * grad_soft, axis=-1, keepdims=True)
            grad_scores = (soft * (grad_soft - delta)).astype(LOW)
            grad_query = grad_query + dot(grad_scores, keys * mask)
            grad_key = grad_key + dot_w(grad_scores, own_query)
            grad_value = grad_value + dot_w(soft.astype(LOW), own_grad)
        grad_query = grad_query * 0.125
        grad_proj[here, :width] = grad_query.astype(LOW)
        totals[0:1] = totals[0:1] + jnp.sum(grad_query, axis=0, keepdims=True)
        acc[0] = acc[0] + grad_key
        acc[1] = acc[1] + grad_value
        return carry

    lax.fori_loop(0, qkv.shape[0] // QUERY_BLOCK, block, 0)
    grad_proj[:, width : 2 * width] = (acc[0] * 0.125).astype(LOW)
    grad_proj[:, 2 * width :] = acc[1].astype(LOW)
    totals[1:2] = jnp.sum(acc[1], axis=0, keepdims=True)


def attend(heads, width, slopes, qkv, marks_column, marks_row):
    length = qkv.shape[0]
    return pl.pallas_call(
        lambda *refs: attend_kernel(heads, width, *refs),
        out_shape=(
            jax.ShapeDtypeStruct((length, width), LOW),
            jax.ShapeDtypeStruct((length, heads), WIDE),
        ),
        in_specs=[pl.BlockSpec(memory_space=pltpu.SMEM)]
        + [pl.BlockSpec(memory_space=pltpu.VMEM)] * 3,
        out_specs=[pl.BlockSpec(memory_space=pltpu.VMEM)] * 2,
        name="attend",
    )(slopes, qkv, marks_column, marks_row)


def attend_back(heads, width, slopes, qkv, grad_out, sums, marks_column, marks_row):
    length = qkv.shape[0]
    return pl.pallas_call(
        lambda *refs: attend_back_kernel(heads, width, *refs),
        out_shape=(
            jax.ShapeDtypeStruct((length, 3 * width), LOW),
            jax.ShapeDtypeStruct((8, width), WIDE),
        ),
        in_specs=[pl.BlockSpec(memory_space=pltpu.SMEM)]
        + [pl.BlockSpec(memory_space=pltpu.VMEM)] * 5,
        out_specs=[pl.BlockSpec(memory_space=pltpu.VMEM)] * 2,
        scratch_shapes=[pltpu.VMEM((2, length, width), WIDE)],
        name="attend_back",
    )(slopes, qkv, grad_out, sums, marks_column, marks_row)


def norm_forward(resid, norm_gain, norm_bias):
    centre = resid - jnp.mean(resid, axis=-1, keepdims=True)
    inverse = lax.rsqrt(jnp.mean(centre * centre, axis=-1, keepdims=True) + EPSILON)
    normed = centre * inverse
    return (normed * norm_gain + norm_bias, normed, inverse)


def norm_backward(grad_rows, normed, inverse, norm_gain):
    scaled = grad_rows * norm_gain
    first_mean = jnp.mean(scaled, axis=-1, keepdims=True)
    second_mean = jnp.mean(scaled * normed, axis=-1, keepdims=True)
    return inverse * (scaled - first_mean - normed * second_mean)


def split_store(kept, sent, block, value):
    if block % 2:
        sent[block // 2] = value.astype(LOW)
    else:
        kept[block // 2] = value


def mlp_kernel(hidden, rows, gate_up_own, down_own, kept, sent, activated, through_gate, through_up):
    for block in range(GROUP):
        here = pl.ds(block * (rows.shape[0] // GROUP), rows.shape[0] // GROUP)
        gate_up = dot(rows[here, :], gate_up_own[...])
        gate, up = gate_up[:, :hidden], gate_up[:, hidden:]
        below = 0.5 * (1.0 + lax.erf(gate * math.sqrt(0.5)))
        density = jnp.exp(-0.5 * gate * gate) * (1.0 / math.sqrt(2.0 * math.pi))
        gelu = gate * below
        low = (gelu * up).astype(LOW)
        activated[here, :] = low
        through_gate[here, :] = up * (below + gate * density)
        through_up[here, :] = gelu
        split_store(kept, sent, block, dot(low, down_own[...]))


def mlp_back_kernel(
    hidden, grads, through_gate, through_up, gate_up_own, down_own, kept, sent, grad_gate_up
):
    grad_activated = dot_t(grads[...], down_own[...])
    grad_gate_up[:, :hidden] = (grad_activated * through_gate[...]).astype(LOW)
    grad_gate_up[:, hidden:] = (grad_activated * through_up[...]).astype(LOW)
    partial = dot_t(grad_gate_up[...], gate_up_own[...])
    count = grads.shape[0] // GROUP
    for block in range(GROUP):
        split_store(kept, sent, block, partial[block * count : (block + 1) * count])


def in_vmem(kernel, out_shape, *arrays):
    return pl.pallas_call(
        kernel,
        out_shape=out_shape,
        in_specs=[pl.BlockSpec(memory_space=pltpu.VMEM)] * len(arrays),
        out_specs=jax.tree.map(lambda _: pl.BlockSpec(memory_space=pltpu.VMEM), out_shape),
    )(*arrays)


def split_shapes(count):
    half = (GROUP // 2, count // GROUP, D)
    return jax.ShapeDtypeStruct(half, WIDE), jax.ShapeDtypeStruct(half, LOW)


def mlp_forward(rows, gate_up_own, down_own):
    count, hidden = rows.shape[0], down_own.shape[0]
    out_shape = split_shapes(count) + (
        jax.ShapeDtypeStruct((count, hidden), LOW),
        jax.ShapeDtypeStruct((count, hidden), WIDE),
        jax.ShapeDtypeStruct((count, hidden), WIDE),
    )
    kernel = lambda *refs: mlp_kernel(hidden, *refs)
    return in_vmem(kernel, out_shape, rows, gate_up_own, down_own)


def mlp_backward(grads, through_gate, through_up, gate_up_own, down_own):
    count, hidden = grads.shape[0], down_own.shape[0]
    out_shape = split_shapes(count) + (jax.ShapeDtypeStruct((count, 2 * hidden), LOW),)
    kernel = lambda *refs: mlp_back_kernel(hidden, *refs)
    arrays = (grads, through_gate, through_up, gate_up_own, down_own)
    return in_vmem(kernel, out_shape, *arrays)


def exchange(value):
    return lax.all_to_all(value, "seq", 0, 0)


def together(*values):
    return lax.optimization_barrier(values)


def local(
    tokens, segments, padding, w_qkv, w_out, w_gate_up, w_down, biases, norm_gains, cotangent
):
    sequences, seq_rows = tokens.shape[:2]
    seq_count, dp_count = lax.axis_size("seq"), lax.axis_size("dp")
    seq_at, dp_at = lax.axis_index("seq"), lax.axis_index("dp")
    halves = seq_count // GROUP
    half_at = seq_at // GROUP
    rows = sequences * seq_rows
    length = seq_count * seq_rows
    head_groups = seq_count // sequences
    heads = -(-H // head_groups)
    padded = heads * head_groups
    width = heads * HD
    own_seq, own_heads = seq_at // head_groups, seq_at % head_groups
    wide_rows = w_qkv.shape[0]
    down_rows = w_down.shape[0]
    bias_part, gain_part = biases.shape[0], norm_gains.shape[0]
    run = dp_count * down_rows

    tokens_flat = tokens.reshape(rows, D)

    by_heads = w_qkv.reshape(wide_rows, 3, H, HD)
    by_heads = jnp.pad(by_heads, ((0, 0), (0, 0), (0, padded - H), (0, 0)))
    by_heads = by_heads.reshape(wide_rows, 3, head_groups, width).transpose(2, 0, 1, 3)
    by_heads = by_heads.reshape(1, head_groups, wide_rows, 3 * width)
    by_heads = jnp.broadcast_to(by_heads, (sequences,) + by_heads.shape[1:])
    by_heads = by_heads.reshape(seq_count, wide_rows, 3 * width)
    small_columns = (bias_part + gain_part) // wide_rows
    small = jnp.concatenate([biases, norm_gains]).reshape(1, wide_rows, small_columns)
    small = jnp.broadcast_to(small, (seq_count, wide_rows, small_columns))
    qkv_rows = exchange(jnp.concatenate([by_heads, small], axis=-1))
    qkv_rows, gate_up_in, down_in = together(qkv_rows, w_gate_up, w_down)
    qkv_own = gather_by_swaps(qkv_rows, "dp", dp_count, dp_at, 1)

    marks = jnp.concatenate([segments, padding], axis=1).astype(LOW)
    extra_rows = -(-marks.shape[1] // (8 * D)) * 8
    marks = jnp.pad(marks, ((0, 0), (0, extra_rows * D - marks.shape[1])))
    packed = jnp.concatenate([tokens, marks.reshape(sequences, extra_rows, D)], axis=1)
    line = put(
        jnp.zeros_like(packed), lax.dynamic_index_in_dim(packed, own_seq, 0, False), own_seq, 0
    )
    for mask in range(1, sequences):
        sent = lax.dynamic_index_in_dim(packed, own_seq ^ mask, 0, False)
        line = put(line, swap(sent, "seq", seq_count, mask * head_groups), own_seq ^ mask, 0)
    line = line_gather(line, head_groups // 2, seq_count, seq_at)
    token_rows = line[:, :seq_rows].reshape(length, D)
    mark_line = line[:, seq_rows:].reshape(seq_count, extra_rows * D)[:, : 2 * seq_rows]
    mark_line = mark_line.reshape(seq_count, 2, seq_rows).astype(WIDE)
    marks_row = jnp.stack([mark_line[:, 0].reshape(length), mark_line[:, 1].reshape(length)])
    marks_column = marks_row.T

    out_part = gather_by_swaps(w_out, "dp", dp_count, dp_at, 0).reshape(-1, D)
    out_full = line_gather(out_part[None], seq_count // 2, seq_count, seq_at).reshape(-1, D)

    columns = gate_up_in.reshape(wide_rows, 2, halves, GROUP, run).transpose(3, 0, 1, 2, 4)
    columns = columns.reshape(1, GROUP, wide_rows, 2 * halves * run)
    columns = jnp.broadcast_to(columns, (halves,) + columns.shape[1:])
    hidden = halves * run
    gate_up_rows = exchange(columns.reshape(seq_count, wide_rows, 2 * hidden))
    gate_up_pieces = swapped(gate_up_rows, "dp", dp_count)
    down_part = gather_by_swaps(down_in, "seq", halves, half_at, 0, GROUP)
    down_pieces = swapped(down_part, "dp", dp_count)

    vectors = qkv_own[..., 3 * width :].reshape(seq_count, dp_count, bias_part + gain_part)
    bias_vector = vectors[:, :, :bias_part].reshape(6 * D).astype(WIDE)
    gain_vector = vectors[:, :, bias_part:].reshape(2 * D).astype(WIDE)
    qkv_own = qkv_own[..., : 3 * width].reshape(D, 3 * width)

    def own_part(vector):
        spread = jnp.pad(vector, (0, padded * HD - D))
        return lax.dynamic_slice_in_dim(spread, own_heads * width, width, 0)

    own_bias = jnp.concatenate(
        [own_part(bias_vector[0:D]), jnp.zeros((width,), WIDE), own_part(bias_vector[D : 2 * D])]
    )
    qkv = (dot(token_rows, qkv_own) + own_bias).astype(LOW)
    slopes = jnp.pad(jnp.asarray(slope_table(H)), (0, padded - H))
    slopes = lax.dynamic_slice_in_dim(slopes, own_heads * heads, heads, 0)
    blended, log_sums = attend(heads, width, slopes, qkv, marks_column, marks_row)
    blended, down_pieces = together(blended, down_pieces)
    down_own = in_order(down_pieces, dp_at, 1).reshape(hidden, D)
    blended = blended.reshape(seq_count, seq_rows, width)

    def to_rows(by_head):
        arrived = exchange(by_head).reshape(sequences, head_groups, seq_rows, -1, width)
        arrived = arrived.transpose(0, 2, 3, 1, 4).reshape(rows, -1, padded * HD)
        return arrived[:, :, :D].reshape(rows, -1)

    attended = to_rows(blended)
    attended, bias_parts, gain_parts = together(
        attended, jnp.split(bias_vector, 6), jnp.split(gain_vector, 2)
    )
    token_wide = tokens_flat.astype(WIDE)
    resid_one = token_wide + (dot(attended, out_full) + bias_parts[2])
    resid_one, gate_up_pieces = together(resid_one, gate_up_pieces)
    gate_up_own = in_order(gate_up_pieces, dp_at, 1).reshape(D, 2 * hidden)
    hidden_one, normed_one, inverse_one = norm_forward(
        resid_one, gain_parts[0], bias_parts[4]
    )
    hidden_rows = group_gather(hidden_one.astype(LOW), seq_count)
    kept, sent, activated, through_gate, through_up = mlp_forward(
        hidden_rows, gate_up_own, down_own
    )
    mlp_out = group_scatter(kept, sent, seq_count)
    resid_two = hidden_one + (mlp_out + bias_parts[3])
    normed_out, normed_two, inverse_two = norm_forward(
        resid_two, gain_parts[1], bias_parts[5]
    )
    valid_mask = padding.reshape(rows, 1).astype(WIDE)
    layer_out = (normed_out * valid_mask).astype(LOW)

    grad_final = cotangent.reshape(rows, D).astype(WIDE) * valid_mask
    grad_gain_two = jnp.sum(grad_final * normed_two, axis=0)
    grad_bias_two = jnp.sum(grad_final, axis=0)
    grad_resid_two = norm_backward(grad_final, normed_two, inverse_two, gain_parts[1])
    grad_bias_down = jnp.sum(grad_resid_two, axis=0)
    grad_mlp_rows = group_gather(grad_resid_two.astype(LOW), seq_count)
    kept, sent, grad_gate_up_low = mlp_backward(
        grad_mlp_rows, through_gate, through_up, gate_up_own, down_own
    )
    grad_hidden = grad_resid_two + group_scatter(kept, sent, seq_count)
    grad_down = dot_w(activated, grad_mlp_rows)
    grad_gate_up = dot_w(hidden_rows, grad_gate_up_low)
    grad_gate_up = grad_gate_up.reshape(seq_count, dp_count, wide_rows, 2 * hidden)
    grad_gate_up = scatter_swaps(grad_gate_up, "dp", dp_count, dp_at, 1)
    shard_down = grad_down.reshape(halves, dp_count, down_rows, D)
    shard_down = scatter_by_swaps(shard_down, "dp", dp_count, dp_at, 1)
    shard_down = scatter_by_swaps(shard_down, "seq", halves, half_at, 0, GROUP)

    grad_gain_one = jnp.sum(grad_hidden * normed_one, axis=0)
    grad_bias_one = jnp.sum(grad_hidden, axis=0)
    grad_resid_one = norm_backward(grad_hidden, normed_one, inverse_one, gain_parts[0])
    grad_bias_attn = jnp.sum(grad_resid_one, axis=0)
    grad_attn_low = grad_resid_one.astype(LOW)
    grad_attended = dot_t(grad_attn_low, out_full).astype(LOW)
    grad_out_w = dot_w(attended, grad_attn_low)
    grad_out_w = grad_out_w.reshape(seq_count, dp_count, wide_rows, D)
    grad_out_w = scatter_swaps(grad_out_w, "dp", dp_count, dp_at, 1)

    spread = grad_attended.reshape(sequences, seq_rows, D)
    spread = jnp.pad(spread, ((0, 0), (0, 0), (0, padded * HD - D)))
    spread = spread.reshape(sequences, seq_rows, head_groups, width).transpose(0, 2, 1, 3)
    grad_blended = exchange(spread.reshape(seq_count, seq_rows, width))
    grad_gate_up = add_up(grad_gate_up).astype(LOW)
    grad_blended = grad_blended.reshape(length, width)
    grad_proj, totals = attend_back(
        heads, width, slopes, qkv, grad_blended, log_sums, marks_column, marks_row
    )

    def whole_part(vector):
        spread = jnp.zeros((padded * HD,), WIDE)
        return lax.dynamic_update_slice(spread, vector, (own_heads * width,))[:D]

    grad_bias_query = whole_part(totals[0])
    grad_bias_value = whole_part(totals[1])
    grad_rows = dot_t(grad_proj, qkv_own).astype(LOW).reshape(seq_count, seq_rows, D)
    grad_rows = sequence_reduce(grad_rows, seq_count, seq_at, sequences)
    grad_qkv = dot_w(token_rows, grad_proj)

    early = exchange(grad_gate_up).astype(WIDE)
    shard_gate_up = early.reshape(halves, GROUP, wide_rows, 2 * hidden)
    shard_gate_up = jnp.sum(shard_gate_up, axis=0).reshape(GROUP, wide_rows, 2, halves, run)
    shard_gate_up = shard_gate_up.transpose(1, 2, 3, 0, 4).reshape(wide_rows, 2 * FF)

    grad_biases = jnp.concatenate(
        [
            grad_bias_query,
            grad_bias_value,
            grad_bias_attn,
            grad_bias_down,
            grad_bias_one,
            grad_bias_two,
        ]
    ).astype(LOW).reshape(seq_count, dp_count, bias_part)
    grad_gains = jnp.concatenate([grad_gain_one, grad_gain_two]).astype(LOW)
    grad_gains = grad_gains.reshape(seq_count, dp_count, gain_part)
    grad_small = jnp.concatenate([grad_biases, grad_gains], axis=-1)
    grad_small = grad_small.reshape(seq_count, dp_count, wide_rows, small_columns)
    late = jnp.concatenate(
        [grad_qkv.reshape(seq_count, dp_count, wide_rows, 3 * width), grad_small], axis=-1
    )
    late = scatter_swaps(late, "dp", dp_count, dp_at, 1)
    late, grad_out_w = together(late, grad_out_w)
    late, grad_out_w = add_up(late).astype(LOW), add_up(grad_out_w).astype(LOW)
    grad_rows = sequence_swap(grad_rows, seq_count, seq_at, sequences)
    grad_tokens = grad_resid_one + grad_rows.reshape(rows, D)
    late = jnp.concatenate([late, grad_out_w], axis=-1)
    late = exchange(late).astype(WIDE)
    small_end = 3 * width + small_columns
    shard_small = jnp.sum(late[:, :, 3 * width : small_end], axis=0).reshape(-1)
    shard_out = jnp.sum(late[:, :, small_end:], axis=0)
    shard_qkv = late[:, :, : 3 * width].reshape(sequences, head_groups, wide_rows, 3, width)
    shard_qkv = jnp.sum(shard_qkv, axis=0).transpose(1, 2, 0, 3)
    shard_qkv = shard_qkv.reshape(wide_rows, 3, padded * HD)[:, :, :D].reshape(wide_rows, 3 * D)

    shape = (sequences, seq_rows, D)
    return (
        layer_out.reshape(shape),
        grad_tokens.reshape(shape),
        shard_qkv,
        shard_out,
        shard_gate_up,
        shard_down,
        shard_small[:bias_part],
        shard_small[bias_part:],
    )


def solution(mesh):
    in_specs = (
        P("dp", "seq", None),
        P("dp", "seq"),
        P("dp", "seq"),
        P(("seq", "dp"), None),
        P(("seq", "dp"), None),
        P(("seq", "dp"), None),
        P(("seq", "dp"), None),
        P(("seq", "dp")),
        P(("seq", "dp")),
        P("dp", "seq", None),
    )
    out_specs = (
        P("dp", "seq", None),
        P("dp", "seq", None),
        P(("seq", "dp"), None),
        P(("seq", "dp"), None),
        P(("seq", "dp"), None),
        P(("seq", "dp"), None),
        P(("seq", "dp")),
        P(("seq", "dp")),
    )

    return jax.shard_map(local, mesh=mesh, in_specs=in_specs, out_specs=out_specs, check_vma=False)
```

```python
import math

import jax
import jax.numpy as jnp
import numpy as np
from jax import lax
from jax.experimental import pallas as pl
from jax.experimental.pallas import tpu as pltpu
from jax.sharding import PartitionSpec as P


D = 768
H = 12
HD = 64
FF = 3072
GROUP = 4
QUERY_BLOCK = 128

SEQ = "seq"
DP = "dp"
NEG_FILL = -1e30
EPSILON = 1e-12
LOW = jnp.bfloat16
WIDE = jnp.float32


def slope_table(head_count):
    nearest = 2 ** int(math.floor(math.log2(head_count)))
    leading = [2.0 ** (-8.0 * (counter + 1) / nearest) for counter in range(nearest)]
    further = [2.0 ** (-8.0 * (counter + 1) / (2 * nearest)) for counter in range(2 * nearest)]
    return np.array(leading + further[0::2][: head_count - nearest], np.float32)


def dot(left, right):
    return jnp.dot(left, right, preferred_element_type=WIDE)


def dot_t(left, right):
    return lax.dot_general(left, right, (((1,), (1,)), ((), ())), preferred_element_type=WIDE)


def dot_w(left, right):
    return lax.dot_general(left, right, (((0,), (0,)), ((), ())), preferred_element_type=WIDE)


def swap(value, axis, size, mask):
    return lax.ppermute(value, axis, [(i, i ^ mask) for i in range(size)])


def put(buffer, value, index, axis):
    starts = [0] * buffer.ndim
    starts[axis] = index
    return lax.dynamic_update_slice(buffer, jnp.expand_dims(value, axis), starts)


def swapped(value, name, size, step=1):
    total = lax.axis_size(name)
    return (value,) + tuple(swap(value, name, total, mask * step) for mask in range(1, size))


def in_order(pieces, place, axis):
    value = pieces[0]
    shape = value.shape[:axis] + (len(pieces),) + value.shape[axis:]
    result = jnp.zeros(shape, value.dtype)
    for mask, piece in enumerate(pieces):
        result = put(result, piece, place ^ mask, axis)
    return result


def gather_by_swaps(value, name, size, place, axis, step=1):
    return in_order(swapped(value, name, size, step), place, axis)


def scatter_swaps(value, name, size, place, axis, step=1):
    total = lax.axis_size(name)
    pieces = [lax.dynamic_index_in_dim(value, place, axis, False)]
    for mask in range(1, size):
        part = lax.dynamic_index_in_dim(value, place ^ mask, axis, False).astype(LOW)
        pieces.append(swap(part, name, total, mask * step))
    return tuple(pieces)


def line_gather(blocks, reach, seq_count, seq_at):
    while reach:
        came = swap(blocks, SEQ, seq_count, reach)
        upper = (seq_at // reach) % 2 == 1
        pair = (jnp.where(upper, came, blocks), jnp.where(upper, blocks, came))
        blocks = jnp.stack(pair, axis=1).reshape((2 * blocks.shape[0],) + blocks.shape[1:])
        reach = reach // 2
    return blocks


def add_up(pieces):
    result = pieces[0].astype(WIDE)
    for piece in pieces[1:]:
        result = result + piece.astype(WIDE)
    return result


def scatter_by_swaps(value, name, size, place, axis, step=1):
    return add_up(scatter_swaps(value, name, size, place, axis, step))


def group_gather(rows, seq_count):
    partner = swap(rows, SEQ, seq_count, 1)
    across = swap(rows, SEQ, seq_count, 2)
    corner = swap(across, SEQ, seq_count, 1)
    return jnp.concatenate([rows, partner, across, corner], axis=0)


def group_scatter(kept, sent, seq_count):
    came = swap(sent, SEQ, seq_count, 1).astype(WIDE)
    across = swap((kept[1] + came[1]).astype(LOW), SEQ, seq_count, 2).astype(WIDE)
    return kept[0] + came[0] + across


def sequence_reduce(blocks, seq_count, seq_at, sequences):
    total, step = blocks, 1
    while total.shape[0] > sequences:
        halves = total.reshape((total.shape[0] // 2, 2) + total.shape[1:])
        bit = (seq_at // step) % 2
        sent = lax.dynamic_index_in_dim(halves, 1 - bit, 1, False).astype(LOW)
        kept = lax.dynamic_index_in_dim(halves, bit, 1, False).astype(WIDE)
        total = kept + swap(sent, SEQ, seq_count, step).astype(WIDE)
        step *= 2
    return total


def sequence_swap(total, seq_count, seq_at, sequences):
    step = seq_count // sequences
    own = seq_at // step
    result = put(jnp.zeros_like(total), lax.dynamic_index_in_dim(total, own, 0, False), own, 0)
    for mask in range(1, sequences):
        sent = lax.dynamic_index_in_dim(total, own ^ mask, 0, False).astype(LOW)
        came = swap(sent, SEQ, seq_count, mask * step).astype(WIDE)
        result = put(result, came, own ^ mask, 0)
    return result


def head_columns(head, width):
    column = lax.broadcasted_iota(jnp.int32, (1, width), 1)
    return ((column >= head * HD) & (column < (head + 1) * HD)).astype(WIDE).astype(LOW)


def block_scores(query_rows, keys, slope, start, marks_column, marks_row):
    shape = (query_rows.shape[0], keys.shape[0])
    row = lax.broadcasted_iota(jnp.int32, shape, 0) + start
    column = lax.broadcasted_iota(jnp.int32, shape, 1)
    distance = jnp.abs(row - column).astype(WIDE)
    allowed = (marks_column[:, 0:1] == marks_row[0:1]) & (marks_row[1:2] >= marks_column[:, 1:2])
    return jnp.where(allowed, dot_t(query_rows, keys) * 0.125 - slope * distance, NEG_FILL)


def attend_kernel(heads, width, slopes, qkv, marks_column, marks_row, out, sums):
    keys, values = qkv[:, width : 2 * width], qkv[:, 2 * width :]

    def block(index, carry):
        start = pl.multiple_of(index * QUERY_BLOCK, QUERY_BLOCK)
        here = pl.ds(start, QUERY_BLOCK)
        queries, marks = qkv[here, :width], marks_column[here, :]
        blended = jnp.zeros((QUERY_BLOCK, width), WIDE)
        for head in range(heads):
            mask = head_columns(head, width)
            scores = block_scores(queries * mask, keys, slopes[head], start, marks, marks_row[...])
            top_score = jnp.max(scores, axis=-1, keepdims=True)
            exponent = jnp.exp(scores - top_score)
            total = jnp.sum(exponent, axis=-1, keepdims=True)
            blended = blended + dot((exponent / total).astype(LOW), values * mask)
            sums[here, head : head + 1] = top_score + jnp.log(total)
        out[here, :] = blended.astype(LOW)
        return carry

    lax.fori_loop(0, qkv.shape[0] // QUERY_BLOCK, block, 0)


def attend_back_kernel(
    heads, width, slopes, qkv, grad_out, sums, marks_column, marks_row, grad_proj, totals, acc
):
    keys, values = qkv[:, width : 2 * width], qkv[:, 2 * width :]
    acc[...] = jnp.zeros(acc.shape, WIDE)
    totals[...] = jnp.zeros(totals.shape, WIDE)

    def block(index, carry):
        start = pl.multiple_of(index * QUERY_BLOCK, QUERY_BLOCK)
        here = pl.ds(start, QUERY_BLOCK)
        queries, marks, grads = qkv[here, :width], marks_column[here, :], grad_out[here, :]
        grad_query = jnp.zeros((QUERY_BLOCK, width), WIDE)
        grad_key = jnp.zeros((qkv.shape[0], width), WIDE)
        grad_value = jnp.zeros((qkv.shape[0], width), WIDE)
        for head in range(heads):
            mask = head_columns(head, width)
            own_query, own_grad = queries * mask, grads * mask
            scores = block_scores(own_query, keys, slopes[head], start, marks, marks_row[...])
            soft = jnp.exp(scores - sums[here, head : head + 1])
            grad_soft = dot_t(own_grad, values)
            delta = jnp.sum(soft * grad_soft, axis=-1, keepdims=True)
            grad_scores = (soft * (grad_soft - delta)).astype(LOW)
            grad_query = grad_query + dot(grad_scores, keys * mask)
            grad_key = grad_key + dot_w(grad_scores, own_query)
            grad_value = grad_value + dot_w(soft.astype(LOW), own_grad)
        grad_query = grad_query * 0.125
        grad_proj[here, :width] = grad_query.astype(LOW)
        totals[0:1] = totals[0:1] + jnp.sum(grad_query, axis=0, keepdims=True)
        acc[0] = acc[0] + grad_key
        acc[1] = acc[1] + grad_value
        return carry

    lax.fori_loop(0, qkv.shape[0] // QUERY_BLOCK, block, 0)
    grad_proj[:, width : 2 * width] = (acc[0] * 0.125).astype(LOW)
    grad_proj[:, 2 * width :] = acc[1].astype(LOW)
    totals[1:2] = jnp.sum(acc[1], axis=0, keepdims=True)


def attend(heads, width, slopes, qkv, marks_column, marks_row):
    length = qkv.shape[0]
    return pl.pallas_call(
        lambda *refs: attend_kernel(heads, width, *refs),
        out_shape=(
            jax.ShapeDtypeStruct((length, width), LOW),
            jax.ShapeDtypeStruct((length, heads), WIDE),
        ),
        in_specs=[pl.BlockSpec(memory_space=pltpu.SMEM)]
        + [pl.BlockSpec(memory_space=pltpu.VMEM)] * 3,
        out_specs=[pl.BlockSpec(memory_space=pltpu.VMEM)] * 2,
        name="at",
    )(slopes, qkv, marks_column, marks_row)


def attend_back(heads, width, slopes, qkv, grad_out, sums, marks_column, marks_row):
    length = qkv.shape[0]
    return pl.pallas_call(
        lambda *refs: attend_back_kernel(heads, width, *refs),
        out_shape=(
            jax.ShapeDtypeStruct((length, 3 * width), LOW),
            jax.ShapeDtypeStruct((8, width), WIDE),
        ),
        in_specs=[pl.BlockSpec(memory_space=pltpu.SMEM)]
        + [pl.BlockSpec(memory_space=pltpu.VMEM)] * 5,
        out_specs=[pl.BlockSpec(memory_space=pltpu.VMEM)] * 2,
        scratch_shapes=[pltpu.VMEM((2, length, width), WIDE)],
        name="ab",
    )(slopes, qkv, grad_out, sums, marks_column, marks_row)


def norm_forward(resid, norm_gain, norm_bias):
    centre = resid - jnp.mean(resid, axis=-1, keepdims=True)
    inverse = lax.rsqrt(jnp.mean(centre * centre, axis=-1, keepdims=True) + EPSILON)
    normed = centre * inverse
    return (normed * norm_gain + norm_bias, normed, inverse)


def norm_backward(grad_rows, normed, inverse, norm_gain):
    scaled = grad_rows * norm_gain
    first_mean = jnp.mean(scaled, axis=-1, keepdims=True)
    second_mean = jnp.mean(scaled * normed, axis=-1, keepdims=True)
    return inverse * (scaled - first_mean - normed * second_mean)


def split_store(kept, sent, block, value):
    if block % 2:
        sent[block // 2] = value.astype(LOW)
    else:
        kept[block // 2] = value


def mlp_kernel(hidden, rows, gate_up_own, down_own, kept, sent, activated, through_gate, through_up):
    for block in range(GROUP):
        here = pl.ds(block * (rows.shape[0] // GROUP), rows.shape[0] // GROUP)
        gate_up = dot(rows[here, :], gate_up_own[...])
        gate, up = gate_up[:, :hidden], gate_up[:, hidden:]
        below = 0.5 * (1.0 + lax.erf(gate * math.sqrt(0.5)))
        density = jnp.exp(-0.5 * gate * gate) * (1.0 / math.sqrt(2.0 * math.pi))
        gelu = gate * below
        low = (gelu * up).astype(LOW)
        activated[here, :] = low
        through_gate[here, :] = up * (below + gate * density)
        through_up[here, :] = gelu
        split_store(kept, sent, block, dot(low, down_own[...]))


def mlp_back_kernel(
    hidden, grads, through_gate, through_up, gate_up_own, down_own, kept, sent, grad_gate_up
):
    grad_activated = dot_t(grads[...], down_own[...])
    grad_gate_up[:, :hidden] = (grad_activated * through_gate[...]).astype(LOW)
    grad_gate_up[:, hidden:] = (grad_activated * through_up[...]).astype(LOW)
    partial = dot_t(grad_gate_up[...], gate_up_own[...])
    count = grads.shape[0] // GROUP
    for block in range(GROUP):
        split_store(kept, sent, block, partial[block * count : (block + 1) * count])


def in_vmem(kernel, out_shape, *arrays):
    return pl.pallas_call(
        kernel,
        out_shape=out_shape,
        in_specs=[pl.BlockSpec(memory_space=pltpu.VMEM)] * len(arrays),
        out_specs=jax.tree.map(lambda _: pl.BlockSpec(memory_space=pltpu.VMEM), out_shape),
    )(*arrays)


def split_shapes(count):
    half = (GROUP // 2, count // GROUP, D)
    return jax.ShapeDtypeStruct(half, WIDE), jax.ShapeDtypeStruct(half, LOW)


def mlp_forward(rows, gate_up_own, down_own):
    count, hidden = rows.shape[0], down_own.shape[0]
    out_shape = split_shapes(count) + (
        jax.ShapeDtypeStruct((count, hidden), LOW),
        jax.ShapeDtypeStruct((count, hidden), WIDE),
        jax.ShapeDtypeStruct((count, hidden), WIDE),
    )
    kernel = lambda *refs: mlp_kernel(hidden, *refs)
    return in_vmem(kernel, out_shape, rows, gate_up_own, down_own)


def mlp_backward(grads, through_gate, through_up, gate_up_own, down_own):
    count, hidden = grads.shape[0], down_own.shape[0]
    out_shape = split_shapes(count) + (jax.ShapeDtypeStruct((count, 2 * hidden), LOW),)
    kernel = lambda *refs: mlp_back_kernel(hidden, *refs)
    arrays = (grads, through_gate, through_up, gate_up_own, down_own)
    return in_vmem(kernel, out_shape, *arrays)


def exchange(value):
    return lax.all_to_all(value, SEQ, 0, 0)


def together(*values):
    return lax.optimization_barrier(values)


def local(
    tokens, segments, padding, w_qkv, w_out, w_gate_up, w_down, biases, norm_gains, cotangent
):
    sequences, seq_rows = tokens.shape[:2]
    seq_count, dp_count = lax.axis_size(SEQ), lax.axis_size(DP)
    seq_at, dp_at = lax.axis_index(SEQ), lax.axis_index(DP)
    halves = seq_count // GROUP
    half_at = seq_at // GROUP
    rows = sequences * seq_rows
    length = seq_count * seq_rows
    head_groups = seq_count // sequences
    heads = -(-H // head_groups)
    padded = heads * head_groups
    width = heads * HD
    own_seq, own_heads = seq_at // head_groups, seq_at % head_groups
    wide_rows = w_qkv.shape[0]
    down_rows = w_down.shape[0]
    bias_part, gain_part = biases.shape[0], norm_gains.shape[0]
    run = dp_count * down_rows

    tokens_flat = tokens.reshape(rows, D)

    by_heads = w_qkv.reshape(wide_rows, 3, H, HD)
    by_heads = jnp.pad(by_heads, ((0, 0), (0, 0), (0, padded - H), (0, 0)))
    by_heads = by_heads.reshape(wide_rows, 3, head_groups, width).transpose(2, 0, 1, 3)
    by_heads = by_heads.reshape(1, head_groups, wide_rows, 3 * width)
    by_heads = jnp.broadcast_to(by_heads, (sequences,) + by_heads.shape[1:])
    by_heads = by_heads.reshape(seq_count, wide_rows, 3 * width)
    small_columns = (bias_part + gain_part) // wide_rows
    small = jnp.concatenate([biases, norm_gains]).reshape(1, wide_rows, small_columns)
    small = jnp.broadcast_to(small, (seq_count, wide_rows, small_columns))
    qkv_rows = exchange(jnp.concatenate([by_heads, small], axis=-1))
    qkv_rows, gate_up_in, down_in = together(qkv_rows, w_gate_up, w_down)
    qkv_own = gather_by_swaps(qkv_rows, DP, dp_count, dp_at, 1)

    marks = jnp.concatenate([segments, padding], axis=1).astype(LOW)
    extra_rows = -(-marks.shape[1] // (8 * D)) * 8
    marks = jnp.pad(marks, ((0, 0), (0, extra_rows * D - marks.shape[1])))
    packed = jnp.concatenate([tokens, marks.reshape(sequences, extra_rows, D)], axis=1)
    line = put(
        jnp.zeros_like(packed), lax.dynamic_index_in_dim(packed, own_seq, 0, False), own_seq, 0
    )
    for mask in range(1, sequences):
        sent = lax.dynamic_index_in_dim(packed, own_seq ^ mask, 0, False)
        line = put(line, swap(sent, SEQ, seq_count, mask * head_groups), own_seq ^ mask, 0)
    line = line_gather(line, head_groups // 2, seq_count, seq_at)
    token_rows = line[:, :seq_rows].reshape(length, D)
    mark_line = line[:, seq_rows:].reshape(seq_count, extra_rows * D)[:, : 2 * seq_rows]
    mark_line = mark_line.reshape(seq_count, 2, seq_rows).astype(WIDE)
    marks_row = jnp.stack([mark_line[:, 0].reshape(length), mark_line[:, 1].reshape(length)])
    marks_column = marks_row.T

    out_part = gather_by_swaps(w_out, DP, dp_count, dp_at, 0).reshape(-1, D)
    out_full = line_gather(out_part[None], seq_count // 2, seq_count, seq_at).reshape(-1, D)

    columns = gate_up_in.reshape(wide_rows, 2, halves, GROUP, run).transpose(3, 0, 1, 2, 4)
    columns = columns.reshape(1, GROUP, wide_rows, 2 * halves * run)
    columns = jnp.broadcast_to(columns, (halves,) + columns.shape[1:])
    hidden = halves * run
    gate_up_rows = exchange(columns.reshape(seq_count, wide_rows, 2 * hidden))
    gate_up_pieces = swapped(gate_up_rows, DP, dp_count)
    down_part = gather_by_swaps(down_in, SEQ, halves, half_at, 0, GROUP)
    down_pieces = swapped(down_part, DP, dp_count)

    vectors = qkv_own[..., 3 * width :].reshape(seq_count, dp_count, bias_part + gain_part)
    bias_vector = vectors[:, :, :bias_part].reshape(6 * D).astype(WIDE)
    gain_vector = vectors[:, :, bias_part:].reshape(2 * D).astype(WIDE)
    qkv_own = qkv_own[..., : 3 * width].reshape(D, 3 * width)

    def own_part(vector):
        spread = jnp.pad(vector, (0, padded * HD - D))
        return lax.dynamic_slice_in_dim(spread, own_heads * width, width, 0)

    own_bias = jnp.concatenate(
        [own_part(bias_vector[0:D]), jnp.zeros((width,), WIDE), own_part(bias_vector[D : 2 * D])]
    )
    qkv = (dot(token_rows, qkv_own) + own_bias).astype(LOW)
    slopes = jnp.pad(jnp.asarray(slope_table(H)), (0, padded - H))
    slopes = lax.dynamic_slice_in_dim(slopes, own_heads * heads, heads, 0)
    blended, log_sums = attend(heads, width, slopes, qkv, marks_column, marks_row)
    blended, down_pieces = together(blended, down_pieces)
    down_own = in_order(down_pieces, dp_at, 1).reshape(hidden, D)
    blended = blended.reshape(seq_count, seq_rows, width)

    def to_rows(by_head):
        arrived = exchange(by_head).reshape(sequences, head_groups, seq_rows, -1, width)
        arrived = arrived.transpose(0, 2, 3, 1, 4).reshape(rows, -1, padded * HD)
        return arrived[:, :, :D].reshape(rows, -1)

    attended = to_rows(blended)
    attended, bias_parts, gain_parts = together(
        attended, jnp.split(bias_vector, 6), jnp.split(gain_vector, 2)
    )
    token_wide = tokens_flat.astype(WIDE)
    resid_one = token_wide + (dot(attended, out_full) + bias_parts[2])
    resid_one, gate_up_pieces = together(resid_one, gate_up_pieces)
    gate_up_own = in_order(gate_up_pieces, dp_at, 1).reshape(D, 2 * hidden)
    hidden_one, normed_one, inverse_one = norm_forward(
        resid_one, gain_parts[0], bias_parts[4]
    )
    hidden_rows = group_gather(hidden_one.astype(LOW), seq_count)
    kept, sent, activated, through_gate, through_up = mlp_forward(
        hidden_rows, gate_up_own, down_own
    )
    mlp_out = group_scatter(kept, sent, seq_count)
    resid_two = hidden_one + (mlp_out + bias_parts[3])
    normed_out, normed_two, inverse_two = norm_forward(
        resid_two, gain_parts[1], bias_parts[5]
    )
    valid_mask = padding.reshape(rows, 1).astype(WIDE)
    layer_out = (normed_out * valid_mask).astype(LOW)

    grad_final = cotangent.reshape(rows, D).astype(WIDE) * valid_mask
    grad_gain_two = jnp.sum(grad_final * normed_two, axis=0)
    grad_bias_two = jnp.sum(grad_final, axis=0)
    grad_resid_two = norm_backward(grad_final, normed_two, inverse_two, gain_parts[1])
    grad_bias_down = jnp.sum(grad_resid_two, axis=0)
    grad_mlp_rows = group_gather(grad_resid_two.astype(LOW), seq_count)
    kept, sent, grad_gate_up_low = mlp_backward(
        grad_mlp_rows, through_gate, through_up, gate_up_own, down_own
    )
    grad_hidden = grad_resid_two + group_scatter(kept, sent, seq_count)
    grad_down = dot_w(activated, grad_mlp_rows)
    grad_gate_up = dot_w(hidden_rows, grad_gate_up_low)
    grad_gate_up = grad_gate_up.reshape(seq_count, dp_count, wide_rows, 2 * hidden)
    grad_gate_up = scatter_swaps(grad_gate_up, DP, dp_count, dp_at, 1)
    shard_down = grad_down.reshape(halves, dp_count, down_rows, D)
    shard_down = scatter_by_swaps(shard_down, DP, dp_count, dp_at, 1)
    shard_down = scatter_by_swaps(shard_down, SEQ, halves, half_at, 0, GROUP)

    grad_gain_one = jnp.sum(grad_hidden * normed_one, axis=0)
    grad_bias_one = jnp.sum(grad_hidden, axis=0)
    grad_resid_one = norm_backward(grad_hidden, normed_one, inverse_one, gain_parts[0])
    grad_bias_attn = jnp.sum(grad_resid_one, axis=0)
    grad_attn_low = grad_resid_one.astype(LOW)
    grad_attended = dot_t(grad_attn_low, out_full).astype(LOW)
    grad_out_w = dot_w(attended, grad_attn_low)
    grad_out_w = grad_out_w.reshape(seq_count, dp_count, wide_rows, D)
    grad_out_w = scatter_swaps(grad_out_w, DP, dp_count, dp_at, 1)

    spread = grad_attended.reshape(sequences, seq_rows, D)
    spread = jnp.pad(spread, ((0, 0), (0, 0), (0, padded * HD - D)))
    spread = spread.reshape(sequences, seq_rows, head_groups, width).transpose(0, 2, 1, 3)
    grad_blended = exchange(spread.reshape(seq_count, seq_rows, width))
    grad_gate_up = add_up(grad_gate_up).astype(LOW)
    grad_blended = grad_blended.reshape(length, width)
    grad_proj, totals = attend_back(
        heads, width, slopes, qkv, grad_blended, log_sums, marks_column, marks_row
    )

    def whole_part(vector):
        spread = jnp.zeros((padded * HD,), WIDE)
        return lax.dynamic_update_slice(spread, vector, (own_heads * width,))[:D]

    grad_bias_query = whole_part(totals[0])
    grad_bias_value = whole_part(totals[1])
    grad_rows = dot_t(grad_proj, qkv_own).astype(LOW).reshape(seq_count, seq_rows, D)
    grad_rows = sequence_reduce(grad_rows, seq_count, seq_at, sequences)
    grad_qkv = dot_w(token_rows, grad_proj)

    early = exchange(grad_gate_up).astype(WIDE)
    shard_gate_up = early.reshape(halves, GROUP, wide_rows, 2 * hidden)
    shard_gate_up = jnp.sum(shard_gate_up, axis=0).reshape(GROUP, wide_rows, 2, halves, run)
    shard_gate_up = shard_gate_up.transpose(1, 2, 3, 0, 4).reshape(wide_rows, 2 * FF)

    grad_biases = jnp.concatenate(
        [
            grad_bias_query,
            grad_bias_value,
            grad_bias_attn,
            grad_bias_down,
            grad_bias_one,
            grad_bias_two,
        ]
    ).astype(LOW).reshape(seq_count, dp_count, bias_part)
    grad_gains = jnp.concatenate([grad_gain_one, grad_gain_two]).astype(LOW)
    grad_gains = grad_gains.reshape(seq_count, dp_count, gain_part)
    grad_small = jnp.concatenate([grad_biases, grad_gains], axis=-1)
    grad_small = grad_small.reshape(seq_count, dp_count, wide_rows, small_columns)
    late = jnp.concatenate(
        [grad_qkv.reshape(seq_count, dp_count, wide_rows, 3 * width), grad_small], axis=-1
    )
    late = scatter_swaps(late, DP, dp_count, dp_at, 1)
    late, grad_out_w = together(late, grad_out_w)
    late, grad_out_w = add_up(late).astype(LOW), add_up(grad_out_w).astype(LOW)
    grad_rows = sequence_swap(grad_rows, seq_count, seq_at, sequences)
    grad_tokens = grad_resid_one + grad_rows.reshape(rows, D)
    late = jnp.concatenate([late, grad_out_w], axis=-1)
    late = exchange(late).astype(WIDE)
    small_end = 3 * width + small_columns
    shard_small = jnp.sum(late[:, :, 3 * width : small_end], axis=0).reshape(-1)
    shard_out = jnp.sum(late[:, :, small_end:], axis=0)
    shard_qkv = late[:, :, : 3 * width].reshape(sequences, head_groups, wide_rows, 3, width)
    shard_qkv = jnp.sum(shard_qkv, axis=0).transpose(1, 2, 0, 3)
    shard_qkv = shard_qkv.reshape(wide_rows, 3, padded * HD)[:, :, :D].reshape(wide_rows, 3 * D)

    shape = (sequences, seq_rows, D)
    return (
        layer_out.reshape(shape),
        grad_tokens.reshape(shape),
        shard_qkv,
        shard_out,
        shard_gate_up,
        shard_down,
        shard_small[:bias_part],
        shard_small[bias_part:],
    )


def solution(mesh):
    in_specs = (
        P(DP, SEQ, None),
        P(DP, SEQ),
        P(DP, SEQ),
        P((SEQ, DP), None),
        P((SEQ, DP), None),
        P((SEQ, DP), None),
        P((SEQ, DP), None),
        P((SEQ, DP)),
        P((SEQ, DP)),
        P(DP, SEQ, None),
    )
    out_specs = (
        P(DP, SEQ, None),
        P(DP, SEQ, None),
        P((SEQ, DP), None),
        P((SEQ, DP), None),
        P((SEQ, DP), None),
        P((SEQ, DP), None),
        P((SEQ, DP)),
        P((SEQ, DP)),
    )

    return jax.shard_map(local, mesh=mesh, in_specs=in_specs, out_specs=out_specs, check_vma=False)
```
